32 devices in a mesh: row: 4 (over z), bulk: 8 (over y, x, core).
Axes of the slice: x: 2, y: 2, z: 4, core: 2. Of those that a mesh axis runs over, the one named last changes fastest.
Arguments:
- child_inverse: float32 [2, 4096, 4096], P(None, 'row', 'bulk')
- child_rhs: float32 [2, 4096, 256], P(None, 'bulk'), may hold values from -6 to 6
- child_update: float32 [2, 1024, 4096], P(None, 'bulk', 'row'), may hold values from -0.09375 to 0.09375
- targets: int32 [2, 1024], replicated, may hold values from 0 to 8191, as said below
- root_inverse: float32 [8192, 8192], P('row', 'bulk')
- root_rhs: float32 [8192, 256], P('bulk'), may hold values from -6 to 6
Outputs:
- root_solution: float32 [8192, 256], P('bulk')
- child_solution: float32 [2, 4096, 256], P(None, 'bulk')
The draws below stay inside these ranges and needn't reach their ends.
Inputs may be any that keep to these rules, and one draw needn't show every extreme that they name: `targets`: for each child, the 128 update rows k * 128 to (k + 1) * 128 - 1 name at most 32 rows of one owner, the owner of root row t being t // 1024; in every such block some owner is named exactly 32 times. A root row may be named more than once.
All inputs are finite; a program needn't handle non-finite values.
Results may differ from the reference program's by a relative error of at most 0.00007.
Values sent between devices are 32-bit elements; how exact they have to be, the bound alone decides.
A program may use at most 128 MiB of HBM per device.

```python
import math
import jax
import jax.numpy as jnp
from jax import lax

WC = 4096
WR = 8192
R = 256
NL = 128
NU = 1024
RB = 1024
CAP = 32


def lower_inverse(key, width, lead):
    key_off, key_diag = jax.random.split(key)
    positions = jnp.arange(width)
    ordering = positions % 32 * (width // 32) + positions // 32
    below = ordering[:, None] > ordering[None, :]
    diagonal = ordering[:, None] == ordering[None, :]
    spread = jax.random.normal(key_off, lead + (width, width), jnp.float32)
    entries = spread * (0.7 / math.sqrt(width))
    diag_values = jax.random.uniform(key_diag, lead + (width, width), jnp.float32, 0.6, 1.4)
    return jnp.where(below, entries, 0.0) + jnp.where(diagonal, diag_values, 0.0)


def draw_child_inverse(key, part):
    return lower_inverse(jax.random.fold_in(key, 11), WC, (2,)).astype(jnp.float32)


def draw_root_inverse(key, part):
    return lower_inverse(jax.random.fold_in(key, 23), WR, ()).astype(jnp.float32)


def draw_targets(key, part):
    keys = jax.random.split(jax.random.fold_in(key, 37), 4)
    sources = NU // NL
    owners = WR // RB
    slots = owners * CAP
    hot_owner = jax.random.randint(keys[0], (2, sources), 0, owners)
    slot_owner = jnp.arange(slots) // CAP
    scores = jax.random.randint(keys[1], (2, sources, slots), 0, 1048576) * slots + jnp.arange(slots)[None, None, :]
    scores = jnp.where(slot_owner[None, None, :] == hot_owner[:, :, None], jnp.arange(slots)[None, None, :] - slots, scores)
    chosen = jnp.argsort(scores, axis=2, stable=True)[:, :, :NL]
    chosen_owner = chosen // CAP
    order = jax.random.randint(keys[2], (2, sources, NL), 0, 1048576) * NL + jnp.arange(NL)[None, None, :]
    shuffle = jnp.argsort(order, axis=2, stable=True)
    owner_of = jnp.take_along_axis(chosen_owner, shuffle, axis=2)
    within = jax.random.randint(keys[3], (2, sources, NL), 0, RB)
    return (owner_of * RB + within).reshape(2, NU).astype(jnp.int32)


def steps_of(rng, shape, pieces, least, high):
    gain, own = 1.0, jax.random.fold_in(rng, 6)
    for position, parts in pieces:
        steps = jnp.exp(jax.random.uniform(jax.random.fold_in(own, position), (parts,), jnp.float32, least / len(pieces), high / len(pieces)))
        gain = gain * jnp.repeat(steps, shape[position] // parts).reshape([-1 if axis == position else 1 for axis in range(len(shape))])
    return gain


def normal_values(rng, dims, scale, most, shards=(), dtype=jnp.bfloat16):
    drawn = jax.random.normal(rng, dims, jnp.float32) * scale
    if len(shards) > 0:
        drawn = steps_of(rng, dims, shards, -0.22, 0.18) * drawn
    return jnp.clip(drawn, min=-most, max=most).astype(dtype)


def setup_inputs(seed: int = 0) -> dict:
    key_of = jax.random.split(jax.random.key(seed), 7)
    return {
        "child_inverse": draw_child_inverse(jax.random.fold_in(key_of[6], 71), 0),
        "child_rhs": normal_values(key_of[1], (2, WC, R), 1.0, 6.0, ((1, 8),), jnp.float32),
        "child_update": normal_values(key_of[2], (2, NU, WC), WC ** -0.5, 0.09375, ((1, 8), (2, 4)), jnp.float32),
        "targets": draw_targets(jax.random.fold_in(key_of[6], 71), 0),
        "root_inverse": draw_root_inverse(jax.random.fold_in(key_of[6], 71), 0),
        "root_rhs": normal_values(key_of[5], (WR, R), 1.0, 6.0, ((0, 8),), jnp.float32),
    }


def reference(child_inverse, child_rhs, child_update, targets, root_inverse, root_rhs):
    highest = lax.Precision.HIGHEST
    forward_child = jnp.einsum('jab,jbr->jar', child_inverse, child_rhs, precision=highest)
    update = jnp.einsum('jua,jar->jur', child_update, forward_child, precision=highest)
    assembled = jnp.zeros((WR, R), jnp.float32).at[targets.reshape(-1)].add(update.reshape(-1, R))
    forward_root = jnp.dot(root_inverse, root_rhs - assembled, precision=highest)
    root_solution = jnp.dot(root_inverse.T, forward_root, precision=highest)
    fetched = root_solution[targets]
    coupling = jnp.einsum('jua,jur->jar', child_update, fetched, precision=highest)
    child_solution = jnp.einsum('jab,jar->jbr', child_inverse, forward_child - coupling, precision=highest)
    return root_solution, child_solution
```

```python
import functools

import jax
import jax.numpy as jnp
from jax import lax
from jax.experimental import pallas as pl
from jax.experimental.pallas import tpu as pltpu
from jax.sharding import PartitionSpec as P

MESH = pl.DeviceIdType.MESH
CHUNKS = 2
OFFSET = 1
SUBS = 1
PIECES = 4
LANES = 128
f32, bf16, i32 = jnp.float32, jnp.bfloat16, jnp.int32


def split(x):
    high = x.astype(bf16)
    return high, (x - high.astype(f32)).astype(bf16)


def dot(a, b):
    return jnp.dot(a, b, preferred_element_type=f32)


def iota(shape, axis):
    return lax.broadcasted_iota(i32, shape, axis)


def one_hot(hit):
    return jnp.where(hit, 1.0, 0.0).astype(bf16)


def log2(n):
    assert n & (n - 1) == 0
    return n.bit_length() - 1


def kernel(
    nb, nr, dims,
    ci_hbm, crhs_ref, cu_hbm, targets_ref, ri_hbm, rrhs_ref,
    root_out, child_out,
    ci, cu, ri,
    part, pair, add_r, add_s, fc, fr, cp,
    up, upx, fe, fex, bk, bkx, cb, cbx,
    pk1, rv1, pk2, rv2,
    ids, pack, place, spread, pick,
    rhs_w, rhs_x, tmp_t,
    load_sem, ar_s, ar_r, a2a_s, a2a_r, ch_s, ch_r,
):
    bits = log2(nb)
    me = lax.axis_index("bulk")
    row = lax.axis_index("row")
    C = fc.shape[-1]
    cols_a, cols_b, own, rows_a, nl, cap = dims
    orders = (list(range(1, bits)), list(range(1, bits))[::-1])

    loads = [
        pltpu.make_async_copy(ci_hbm, ci, load_sem.at[0]),
        pltpu.make_async_copy(cu_hbm, cu, load_sem.at[1]),
        pltpu.make_async_copy(ri_hbm, ri, load_sem.at[2]),
    ]
    for load in loads:
        load.start()

    def across(bit):
        return me + (1 << bit) * (1 - 2 * ((me // (1 << bit)) % 2))

    right = lax.rem(row + 1, nr)
    left = lax.rem(row + nr - 1, nr)
    barrier = pltpu.get_barrier_semaphore()
    for d in range(1, nb):
        pl.semaphore_signal(barrier, inc=1, device_id={"bulk": lax.rem(me + d, nb)}, device_id_type=MESH)
    for side in (left, right):
        pl.semaphore_signal(barrier, inc=1, device_id={"row": side}, device_id_type=MESH)

    def remote(src, dst, send, recv, **where):
        return pltpu.make_async_remote_copy(
            src_ref=src, dst_ref=dst, send_sem=send, recv_sem=recv, device_id=where, device_id_type=MESH
        )

    pending = [[] for _ in range(CHUNKS)]

    def flush(h):
        for finish in pending[h]:
            finish()
        pending[h] = []

    def all_reduce(h, which, out, produce):
        buf = part
        half = buf.shape[2] // 2
        mine = pl.multiple_of((me % 2) * half, half)
        theirs = pl.multiple_of((1 - me % 2) * half, half)
        sends = []
        size = half // SUBS

        def send(f, step, q, src, dst, bit):
            copy = remote(src, dst, ar_s.at[h, which, f, step, q], ar_r.at[h, which, f, step, q], bulk=across(bit))
            copy.start()
            sends.append(copy.wait_send)
            return copy

        def held(f, step, q):
            if step == 0:
                return buf.at[h, f, pl.ds(pl.multiple_of(mine + q * size, size), size)]
            return add_s.at[h, f, step - 1, pl.ds(q * size, size)]

        def landed(f, step, q):
            return add_r.at[h, f, step, pl.ds(q * size, size)]

        flush(h)
        pairs = []
        for f in range(2):
            produce(f, theirs, half)
            pairs.append(send(f, bits - 1, 0, buf.at[h, f, pl.ds(theirs, half)], pair.at[h, f], 0))
        flights = {}
        for f in range(2):
            produce(f, mine, half)
            pairs[f].wait_recv()
            for q in range(SUBS):
                held(f, 0, q)[...] += pair[h, f, q * size:(q + 1) * size]
                flights[f, q] = send(f, 0, q, held(f, 0, q), landed(f, 0, q), orders[f][0])
        yield
        for step in range(bits - 1):
            for q in range(SUBS):
                for f in range(2):
                    flights[f, q].wait_recv()
                    total = held(f, step, q)[...] + landed(f, step, q)[...]
                    if step == bits - 2:
                        at = out.at[h, f, pl.ds(pl.multiple_of(mine + q * size, size), size)]
                        at[...] = total
                        flights[f, q] = send(f, bits, q, at, at, 0)
                    else:
                        held(f, step + 1, q)[...] = total
                        flights[f, q] = send(
                            f, step + 1, q, held(f, step + 1, q), landed(f, step + 1, q), orders[f][step + 1]
                        )
            yield
        for q in range(SUBS):
            for f in range(2):
                flights[f, q].wait_recv()
        pending[h] += sends

    def exchange(h, which, packed, arrived):
        n = 2 * cap
        here = pl.ds(pl.multiple_of(me * n, n), n)
        copies = []
        for d in range(1, nb):
            peer = lax.rem(me + d, nb)
            copy = remote(
                packed.at[h, pl.ds(pl.multiple_of(peer * n, n), n)], arrived.at[h, here],
                a2a_s.at[h, which, d], a2a_r.at[h, which, d], bulk=peer,
            )
            copy.start()
            copies.append(copy)
        arrived[h, here] = packed[h, here]
        yield
        for copy in copies:
            copy.wait_recv()
        pending[h] += [copy.wait_send for copy in copies]

    def chain(h, which, p, x, produce=None, stride=1):
        pieces = p.shape[1]

        @pl.when(row == 0)
        def _():
            x[h, 0] = jnp.zeros(x.shape[2:], f32)

        @pl.when(row == nr - 1)
        def _():
            x[h, 1] = jnp.zeros(x.shape[2:], f32)

        def flow(side, i, has_source, has_target, target):
            copy = remote(
                x.at[h, 2 + side, i], x.at[h, side, i],
                ch_s.at[h, which, side, i], ch_r.at[h, which, side, i], row=target,
            )

            @pl.when(has_source)
            def _():
                copy.wait_recv()

            @pl.when(has_target)
            def _():
                x[h, 2 + side, i] = x[h, side, i] + p[h, i]
                copy.start()

        for t in range(pieces + nr - 1):
            if t > 0:
                yield
            if produce is not None and t < pieces and t % stride == 0:
                produce(t // stride)
            i = t - row

            @pl.when((i >= 0) & (i < pieces))
            def _():
                flow(0, i, row > 0, row < nr - 1, right)

            k = t - (nr - 1 - row)

            @pl.when((k >= 0) & (k < pieces))
            def _():
                flow(1, k, row < nr - 1, row > 0, left)

        def finish():
            for i in range(pieces):
                for side, has_target, target in ((0, row < nr - 1, right), (1, row > 0, left)):
                    @pl.when(has_target)
                    def _():
                        remote(
                            x.at[h, 2 + side, i], x.at[h, side, i],
                            ch_s.at[h, which, side, i], ch_r.at[h, which, side, i], row=target,
                        ).wait_send()

        pending[h].append(finish)

    def times(a_tile, count, store, h, width, w=rhs_w):
        def body(i, carry):
            high, low = split(a_tile(i))
            both = dot(high, w[h, :width]) + dot(low, w[h, :width])
            store(i, both[:, :C] + both[:, C:])
            return carry

        lax.fori_loop(0, count, body, 0)

    def moved(rows, store, h, width, tile=256):
        tile = min(tile, rows.shape[0])

        def body(i, carry):
            at = pl.ds(pl.multiple_of(i * tile, tile), tile)
            both = dot(rows[at], rhs_w[h, :width])
            store(at, both[:, :C] + both[:, C:])
            return carry

        lax.fori_loop(0, rows.shape[0] // tile, body, 0)

    def keep_right(h, at, value, w=rhs_w):
        high, low = split(value)
        w[h, at, :C] = high
        w[h, at, C:] = low

    def keep_transposed(h, depth, k_tile, y_tile):
        for k in range(depth // k_tile):
            high, low = split(y_tile(k).T)
            tmp_t[h, :C, k * k_tile:(k + 1) * k_tile] = high
            tmp_t[h, C:, k * k_tile:(k + 1) * k_tile] = low

    def transposed_tile(a_tile, depth, k_tile, width, h):
        total = jnp.zeros((2 * C, width), f32)
        for k in range(depth // k_tile):
            high, low = split(a_tile(k))
            y = tmp_t[h, :, k * k_tile:(k + 1) * k_tile]
            total += dot(y, high) + dot(y, low)
        return (total[:C] + total[C:]).T

    def tiles(n, most):
        size = min(n, most)
        return size, n // size

    slots = nb * 2 * cap

    def turned(line):
        return jnp.broadcast_to(line, (LANES, LANES)).T

    def route():
        square = (LANES, LANES)
        before = iota(square, 0) < iota(square, 1)
        ids[...] = jnp.full(ids.shape, -1.0, f32)
        for j in range(2):
            for b in range(nb):
                ids[j * nb + b:j * nb + b + 1, :] = targets_ref[j:j + 1, b * nl:(b + 1) * nl].astype(f32)
        for j in range(2):
            line = ids[pl.ds(j * nb + me, 1), :]
            owner = lax.shift_right_logical(line.astype(i32), log2(own)).astype(f32)
            same = (turned(owner) == owner) & before
            rank = jnp.sum(jnp.where(same, 1.0, 0.0), axis=0, keepdims=True)
            position = owner * (2.0 * cap) + (rank + j * cap)
            column = turned(position).astype(i32)
            at = slice(j * nl, (j + 1) * nl)
            pack[:, at] = one_hot(iota((slots, nl), 0) == position.astype(i32))
            for g in range(slots // LANES):
                place[at, g * LANES:(g + 1) * LANES] = one_hot(iota(square, 1) + g * LANES == column)
        first = (me * own).astype(f32)
        local = ids[...] - first
        inside = (local >= 0.0) & (local < float(own))
        ones = jnp.where(inside, 1.0, 0.0).astype(bf16)
        rank = dot(ones, one_hot(before))
        index = iota(ids.shape, 0)
        child = jnp.where(index >= nb, 1, 0)
        base = (index - nb * child) * (2 * cap) + child * cap
        position = jnp.where(inside, rank + base.astype(f32), -1.0)
        position, local = position.T, local.T
        fill = iota(square, 1).astype(f32)
        lines = []
        for g in range(slots // LANES):
            total = jnp.zeros(square, f32)
            for j in range(2):
                for b in range(nb):
                    if (b * 2 * cap + j * cap) // LANES == g:
                        r = j * nb + b
                        hit = position[:, r:r + 1] == fill + float(g * LANES)
                        total = total + jnp.where(hit, local[:, r:r + 1] + 1.0, 0.0)
            lines.append(jnp.sum(total, axis=0, keepdims=True) - 1.0)
        for g, line in enumerate(lines):
            at = slice(g * LANES, (g + 1) * LANES)
            spread[:, at] = one_hot(iota((own, LANES), 0) == line.astype(i32))
            column = turned(line).astype(i32)
            for k in range(own // LANES):
                pick[at, k * LANES:(k + 1) * LANES] = one_hot(iota(square, 1) + k * LANES == column)

    side = []

    def deliver(h):
        yield from chain(h, 2, bk, bkx)
        size = bk.shape[2]
        for i in range(bk.shape[1]):
            root_out[i * size:(i + 1) * size, h * C:(h + 1) * C] = bkx[h, 0, i] + bk[h, i] + bkx[h, 1, i]

    def program(h):
        lanes = slice(h * C, (h + 1) * C)
        if h == 0:
            pl.semaphore_wait(barrier, nb + 1)
            loads[0].wait()

        def produce1(j, start, length):
            tm, count = tiles(length, 256)
            keep_right(h, slice(0, cols_b), crhs_ref[j, :, lanes])

            def store(i, value):
                part[h, j, pl.ds(pl.multiple_of(start + i * tm, tm), tm)] = value

            times(lambda i: ci[j, pl.ds(pl.multiple_of(start + i * tm, tm), tm), :], count, store, h, cols_b)

        yield from all_reduce(h, 0, fc, produce1)
        if h == 0:
            loads[1].wait()
        for j in range(2):
            keep_right(h, slice(0, cols_a), fc[h, j])

            def store(i, value, j=j):
                up[h, j] = value

            times(lambda i, j=j: cu[j], 1, store, h, cols_a)
        flush(h)
        yield from chain(h, 0, up, upx)
        for j in range(2):
            keep_right(h, slice(j * nl, (j + 1) * nl), upx[h, 0, j] + up[h, j] + upx[h, 1, j])

        def store_packed(at, value):
            pk1[h, at] = value

        moved(pack, store_packed, h, 2 * nl)
        yield from exchange(h, 0, pk1, rv1)
        keep_right(h, slice(0, slots), rv1[h])

        def store_rest(at, value):
            keep_right(h, at, rrhs_ref[at, lanes] - value, rhs_x)

        moved(spread, store_rest, h, slots)
        if h == 0:
            loads[2].wait()
        per = rows_a // 2

        def produce4(f, start, length):
            tm, count = tiles(length, 256)

            def store(i, value):
                part[h, f, pl.ds(pl.multiple_of(start + i * tm, tm), tm)] = value

            times(lambda i: ri[pl.ds(pl.multiple_of(f * per + start + i * tm, tm), tm), :], count, store, h, own, rhs_x)

        yield from all_reduce(h, 1, fr, produce4)
        pieces, size = bk.shape[1], bk.shape[2]
        width = min(256, own)
        kt5, _ = tiles(per, 512)
        halves = per // kt5

        keep_transposed(h, rows_a, kt5, lambda k: fr[h, k // halves, (k % halves) * kt5:(k % halves + 1) * kt5])

        for i in range(own // width):
            value = transposed_tile(
                lambda k: ri[k * kt5:(k + 1) * kt5, i * width:(i + 1) * width], rows_a, kt5, width, h
            )
            for n in range(width // size):
                bk[h, i * (width // size) + n] = value[n * size:(n + 1) * size]
            keep_right(h, slice(i * width, (i + 1) * width), value)
        flush(h)

        def store_picked(at, value):
            pk2[h, at] = value

        moved(pick, store_picked, h, own)
        side.append((h, deliver(h)))
        yield from exchange(h, 1, pk2, rv2)
        keep_right(h, slice(0, slots), rv2[h])

        for j in range(2):
            both = dot(place[j * nl:(j + 1) * nl], rhs_w[h, :slots])
            fe[h, j] = both[:, :C] + both[:, C:]
        yield from chain(h, 1, fe, fex)

        def produce7(j, start, length):
            w7, count7 = tiles(length, 256)
            keep_transposed(h, nl, nl, lambda k: fex[h, 0, j] + fe[h, j] + fex[h, 1, j])

            def body(i, carry):
                at = pl.ds(pl.multiple_of(start + i * w7, w7), w7)
                part[h, j, at] = transposed_tile(lambda k: cu[j, :, at], nl, nl, w7, h)
                return carry

            lax.fori_loop(0, count7, body, 0)

        yield from all_reduce(h, 2, cp, produce7)
        pieces8, size8 = cb.shape[1], cb.shape[2]
        w8, count8 = tiles(cols_b, 256)
        kt8, _ = tiles(cols_a, 512)

        def produce8(n):
            j, i = n // count8, n % count8
            if i == 0:
                keep_transposed(
                    h, cols_a, kt8,
                    lambda k: fc[h, j, k * kt8:(k + 1) * kt8] - cp[h, j, k * kt8:(k + 1) * kt8],
                )
            value = transposed_tile(
                lambda k: ci[j, k * kt8:(k + 1) * kt8, i * w8:(i + 1) * w8], cols_a, kt8, w8, h
            )
            for m in range(w8 // size8):
                cb[h, n * (w8 // size8) + m] = value[m * size8:(m + 1) * size8]

        yield from chain(h, 3, cb, cbx, produce8, w8 // size8)
        for i in range(pieces8):
            j, k = i // (pieces8 // 2), i % (pieces8 // 2)
            child_out[j, k * size8:(k + 1) * size8, lanes] = cbx[h, 0, i] + cb[h, i] + cbx[h, 1, i]

    running = [program(h) for h in range(CHUNKS)]
    turn = 0

    def advance(thread):
        try:
            next(thread)
            return True
        except StopIteration:
            return False

    while any(p is not None for p in running) or side:
        for h in range(CHUNKS):
            if running[h] is not None and turn >= h * OFFSET:
                if not advance(running[h]):
                    running[h] = None
                if turn == 0:
                    route()
            for item in list(side):
                if item[0] == h and not advance(item[1]):
                    side.remove(item)
        turn += 1
    for h in range(CHUNKS):
        flush(h)


def per_device(nb, nr, child_inverse, child_rhs, child_update, targets, root_inverse, root_rhs):
    bits = nb.bit_length() - 1
    _, cols_a, cols_b = child_inverse.shape
    nl = child_update.shape[1]
    rows_a, own = root_inverse.shape
    R = root_rhs.shape[1]
    H, C = CHUNKS, R // CHUNKS
    cap = 2 * nl // nb
    assert rows_a == 2 * cols_a and nl == LANES
    slots = 2 * nb * cap
    root_pieces = min(PIECES, own // 32)
    child_pieces = 2 * min(PIECES // 2, cols_b // 32)
    most = max(root_pieces, child_pieces, 2)
    any_, vmem = pl.BlockSpec(memory_space=pl.ANY), pl.BlockSpec(memory_space=pltpu.VMEM)

    def sums(*dims):
        return pltpu.VMEM((H, 2, *dims, C), f32)

    def chains(pieces, rows):
        return [pltpu.VMEM((H, pieces, rows, C), f32), pltpu.VMEM((H, 4, pieces, rows, C), f32)]

    return pl.pallas_call(
        functools.partial(kernel, nb, nr, (cols_a, cols_b, own, rows_a, nl, cap)),
        out_shape=(
            jax.ShapeDtypeStruct(root_rhs.shape, f32),
            jax.ShapeDtypeStruct(child_rhs.shape, f32),
        ),
        in_specs=[any_, vmem, any_, vmem, any_, vmem],
        out_specs=(vmem, vmem),
        scratch_shapes=[
            pltpu.VMEM(child_inverse.shape, f32),
            pltpu.VMEM(child_update.shape, f32),
            pltpu.VMEM(root_inverse.shape, f32),
            sums(cols_a),
            sums(cols_a // 2),
            sums(bits - 1, cols_a // 2),
            sums(bits - 2, cols_a // 2),
            sums(cols_a),
            sums(rows_a // 2),
            sums(cols_a),
            *chains(2, nl),
            *chains(2, nl),
            *chains(root_pieces, own // root_pieces),
            *chains(child_pieces, 2 * cols_b // child_pieces),
            *[pltpu.VMEM((H, slots, C), f32)] * 4,
            pltpu.VMEM((LANES, LANES), f32),
            pltpu.VMEM((slots, 2 * nl), bf16),
            pltpu.VMEM((2 * nl, slots), bf16),
            pltpu.VMEM((own, slots), bf16),
            pltpu.VMEM((slots, own), bf16),
            pltpu.VMEM((H, max(own, cols_a, cols_b, slots), 2 * C), bf16),
            pltpu.VMEM((H, own, 2 * C), bf16),
            pltpu.VMEM((H, 2 * C, max(rows_a, cols_a, nl)), bf16),
            pltpu.SemaphoreType.DMA((3,)),
            pltpu.SemaphoreType.DMA((H, 3, 2, bits + 1, SUBS)),
            pltpu.SemaphoreType.DMA((H, 3, 2, bits + 1, SUBS)),
            pltpu.SemaphoreType.DMA((H, 2, nb)),
            pltpu.SemaphoreType.DMA((H, 2, nb)),
            pltpu.SemaphoreType.DMA((H, 4, 2, most)),
            pltpu.SemaphoreType.DMA((H, 4, 2, most)),
        ],
        compiler_params=pltpu.CompilerParams(
            collective_id=0, has_side_effects=True, vmem_limit_bytes=62 * 1024 * 1024
        ),
    )(child_inverse, child_rhs, child_update, targets, root_inverse, root_rhs)


def solution(mesh):
    return jax.shard_map(
        functools.partial(per_device, mesh.shape["bulk"], mesh.shape["row"]),
        mesh=mesh,
        in_specs=(
            P(None, "row", "bulk"),
            P(None, "bulk", None),
            P(None, "bulk", "row"),
            P(),
            P("row", "bulk"),
            P("bulk", None),
        ),
        out_specs=(P("bulk", None), P(None, "bulk", None)),
        check_vma=False,
    )
```

```python
import functools

import jax
import jax.numpy as jnp
from jax import lax
from jax.experimental import pallas as pl
from jax.experimental.pallas import tpu as pltpu
from jax.sharding import PartitionSpec as P

MESH = pl.DeviceIdType.MESH
CHUNKS = 2
OFFSET = 2
LATE = (1, 1)
GAP = 1
COPIES = 4
PIECES = 4
LANES = 128
f32, bf16, i32 = jnp.float32, jnp.bfloat16, jnp.int32


def split(x):
    high = x.astype(bf16)
    return high, (x - high.astype(f32)).astype(bf16)


def dot(a, b):
    return jnp.dot(a, b, preferred_element_type=f32)


def iota(shape, axis):
    return lax.broadcasted_iota(i32, shape, axis)


def one_hot(hit):
    return jnp.where(hit, 1.0, 0.0).astype(bf16)


def log2(n):
    assert n & (n - 1) == 0
    return n.bit_length() - 1


def kernel(
    nb, nr, dims,
    ci_hbm, crhs_ref, cu_hbm, targets_ref, ri_hbm, rrhs_ref,
    root_out, child_out,
    ci, cu, ri,
    part, pair, add_r, fc, fr, cp,
    up, upx, fe, fex, bk, bkx, cb, cbx,
    pk1, rv1, pk2, rv2,
    ids, pack, place, spread, pick,
    rhs_w, rhs_x, tmp_t,
    load_sem, ar_s, ar_r, a2a_s, a2a_r, ch_s, ch_r,
):
    bits = log2(nb)
    me = lax.axis_index("bulk")
    row = lax.axis_index("row")
    C = fc.shape[-1]
    cols_a, cols_b, own, rows_a, nl, cap = dims
    orders = (list(range(1, bits)), list(range(1, bits))[::-1])

    loads = [
        pltpu.make_async_copy(ci_hbm, ci, load_sem.at[0]),
        pltpu.make_async_copy(cu_hbm, cu, load_sem.at[1]),
        pltpu.make_async_copy(ri_hbm, ri, load_sem.at[2]),
    ]
    for load in loads:
        load.start()

    def bit_of(bit):
        return (me // (1 << bit)) % 2

    def across(bit):
        return me + (1 << bit) * (1 - 2 * bit_of(bit))

    right = lax.rem(row + 1, nr)
    left = lax.rem(row + nr - 1, nr)
    barrier = pltpu.get_barrier_semaphore()
    for d in range(1, nb):
        pl.semaphore_signal(barrier, inc=1, device_id={"bulk": lax.rem(me + d, nb)}, device_id_type=MESH)
    for side in (left, right):
        pl.semaphore_signal(barrier, inc=1, device_id={"row": side}, device_id_type=MESH)

    def remote(src, dst, send, recv, **where):
        return pltpu.make_async_remote_copy(
            src_ref=src, dst_ref=dst, send_sem=send, recv_sem=recv, device_id=where, device_id_type=MESH
        )

    pending = [[] for _ in range(CHUNKS)]

    def flush(h):
        for finish in pending[h]:
            finish()
        pending[h] = []

    def all_reduce(h, which, out, produce):
        half = part.shape[2] // 2
        mine = pl.multiple_of((me % 2) * half, half)
        theirs = pl.multiple_of((1 - me % 2) * half, half)
        sends = []

        def send(f, step, src, dst, bit):
            copy = remote(src, dst, ar_s.at[h, which, f, step], ar_r.at[h, which, f, step], bulk=across(bit))
            copy.start()
            sends.append(copy.wait_send)
            return copy

        def rows(start, length):
            return pl.ds(pl.multiple_of(start, length), length)

        flush(h)
        pairs = []
        for f in range(2):
            produce(f, theirs, half)
            pairs.append(send(f, 0, part.at[h, f, pl.ds(theirs, half)], pair.at[h, f], 0))
        starts, flights, length, off = [mine, mine], [None, None], half, 0

        def halve(f, step):
            n, bit = length // 2, bit_of(orders[f][step])
            flights[f] = send(
                f, 1 + step, part.at[h, f, rows(starts[f] + (1 - bit) * n, n)], add_r.at[h, f, pl.ds(off, n)],
                orders[f][step],
            )
            starts[f] = starts[f] + bit * n

        for f in range(2):
            produce(f, mine, half)
            pairs[f].wait_recv()
            part[h, f, pl.ds(mine, half)] += pair[h, f]
            halve(f, 0)
        yield
        for step in range(bits - 1):
            length //= 2
            for f in range(2):
                flights[f].wait_recv()
                at = rows(starts[f], length)
                total = part[h, f, at] + add_r[h, f, pl.ds(off, length)]
                if step < bits - 2:
                    part[h, f, at] = total
                    off += length
                    halve(f, step + 1)
                    off -= length
                else:
                    out[h, f, at] = total
                    at = out.at[h, f, at]
                    flights[f] = send(f, bits, at, at, orders[f][step])
            off += length
            yield
        for step in reversed(range(bits - 1)):
            for f in range(2):
                flights[f].wait_recv()
                starts[f] = starts[f] - bit_of(orders[f][step]) * length
                at = out.at[h, f, rows(starts[f], 2 * length)]
                to = orders[f][step - 1] if step > 0 else 0
                flights[f] = send(f, 2 * bits - 1 - step, at, at, to)
            length *= 2
            yield
        for f in range(2):
            flights[f].wait_recv()
        pending[h] += sends

    def exchange(h, which, packed, arrived):
        n = 2 * cap
        here = pl.ds(pl.multiple_of(me * n, n), n)
        copies = []
        for d in range(1, nb):
            peer = lax.rem(me + d, nb)
            copy = remote(
                packed.at[h, pl.ds(pl.multiple_of(peer * n, n), n)], arrived.at[h, here],
                a2a_s.at[h, which, d], a2a_r.at[h, which, d], bulk=peer,
            )
            copy.start()
            copies.append(copy)
        arrived[h, here] = packed[h, here]
        yield
        for copy in copies:
            copy.wait_recv()
        pending[h] += [copy.wait_send for copy in copies]

    def chain(h, which, p, x, produce=None, stride=1):
        pieces = p.shape[1]

        @pl.when(row == 0)
        def _():
            x[h, 0] = jnp.zeros(x.shape[2:], f32)

        @pl.when(row == nr - 1)
        def _():
            x[h, 1] = jnp.zeros(x.shape[2:], f32)

        def flow(side, i, has_source, has_target, target):
            copy = remote(
                x.at[h, 2 + side, i], x.at[h, side, i],
                ch_s.at[h, which, side, i], ch_r.at[h, which, side, i], row=target,
            )

            @pl.when(has_source)
            def _():
                copy.wait_recv()

            @pl.when(has_target)
            def _():
                x[h, 2 + side, i] = x[h, side, i] + p[h, i]
                copy.start()

        for t in range(pieces + nr - 1):
            if t > 0:
                yield
            if produce is not None and t < pieces and t % stride == 0:
                produce(t // stride)
            i = t - row

            @pl.when((i >= 0) & (i < pieces))
            def _():
                flow(0, i, row > 0, row < nr - 1, right)

            k = t - (nr - 1 - row)

            @pl.when((k >= 0) & (k < pieces))
            def _():
                flow(1, k, row < nr - 1, row > 0, left)

        def finish():
            for i in range(pieces):
                for side, has_target, target in ((0, row < nr - 1, right), (1, row > 0, left)):
                    @pl.when(has_target)
                    def _():
                        remote(
                            x.at[h, 2 + side, i], x.at[h, side, i],
                            ch_s.at[h, which, side, i], ch_r.at[h, which, side, i], row=target,
                        ).wait_send()

        pending[h].append(finish)

    def times(a_tile, count, store, h, width, w=rhs_w):
        def body(i, carry):
            high, low = split(a_tile(i))
            both = dot(high, w[h, :width]) + dot(low, w[h, :width])
            store(i, both[:, :C] + both[:, C:])
            return carry

        lax.fori_loop(0, count, body, 0)

    def moved(rows, store, h, width, tile=256):
        tile = min(tile, rows.shape[0])

        def body(i, carry):
            at = pl.ds(pl.multiple_of(i * tile, tile), tile)
            both = dot(rows[at], rhs_w[h, :width])
            store(at, both[:, :C] + both[:, C:])
            return carry

        lax.fori_loop(0, rows.shape[0] // tile, body, 0)

    def keep_right(h, at, value, w=rhs_w):
        high, low = split(value)
        w[h, at, :C] = high
        w[h, at, C:] = low

    def keep_transposed(h, depth, k_tile, y_tile):
        for k in range(depth // k_tile):
            high, low = split(y_tile(k).T)
            tmp_t[h, :C, k * k_tile:(k + 1) * k_tile] = high
            tmp_t[h, C:, k * k_tile:(k + 1) * k_tile] = low

    def transposed_tile(a_tile, depth, k_tile, width, h):
        total = jnp.zeros((2 * C, width), f32)
        for k in range(depth // k_tile):
            high, low = split(a_tile(k))
            y = tmp_t[h, :, k * k_tile:(k + 1) * k_tile]
            total += dot(y, high) + dot(y, low)
        return (total[:C] + total[C:]).T

    def tiles(n, most):
        size = min(n, most)
        return size, n // size

    slots = nb * 2 * cap

    def turned(line):
        return jnp.broadcast_to(line, (LANES, LANES)).T

    def route():
        square = (LANES, LANES)
        before = iota(square, 0) < iota(square, 1)
        ids[...] = jnp.full(ids.shape, -1.0, f32)
        for j in range(2):
            for b in range(nb):
                ids[j * nb + b:j * nb + b + 1, :] = targets_ref[j:j + 1, b * nl:(b + 1) * nl].astype(f32)
        for j in range(2):
            line = ids[pl.ds(j * nb + me, 1), :]
            owner = lax.shift_right_logical(line.astype(i32), log2(own)).astype(f32)
            same = (turned(owner) == owner) & before
            rank = jnp.sum(jnp.where(same, 1.0, 0.0), axis=0, keepdims=True)
            position = owner * (2.0 * cap) + (rank + j * cap)
            column = turned(position).astype(i32)
            at = slice(j * nl, (j + 1) * nl)
            pack[:, at] = one_hot(iota((slots, nl), 0) == position.astype(i32))
            for g in range(slots // LANES):
                place[at, g * LANES:(g + 1) * LANES] = one_hot(iota(square, 1) + g * LANES == column)
        first = (me * own).astype(f32)
        local = ids[...] - first
        inside = (local >= 0.0) & (local < float(own))
        ones = jnp.where(inside, 1.0, 0.0).astype(bf16)
        rank = dot(ones, one_hot(before))
        index = iota(ids.shape, 0)
        child = jnp.where(index >= nb, 1, 0)
        base = (index - nb * child) * (2 * cap) + child * cap
        position = jnp.where(inside, rank + base.astype(f32), -1.0)
        position, local = position.T, local.T
        fill = iota(square, 1).astype(f32)
        lines = []
        for g in range(slots // LANES):
            total = jnp.zeros(square, f32)
            for j in range(2):
                for b in range(nb):
                    if (b * 2 * cap + j * cap) // LANES == g:
                        r = j * nb + b
                        hit = position[:, r:r + 1] == fill + float(g * LANES)
                        total = total + jnp.where(hit, local[:, r:r + 1] + 1.0, 0.0)
            lines.append(jnp.sum(total, axis=0, keepdims=True) - 1.0)
        for g, line in enumerate(lines):
            at = slice(g * LANES, (g + 1) * LANES)
            spread[:, at] = one_hot(iota((own, LANES), 0) == line.astype(i32))
            column = turned(line).astype(i32)
            for k in range(own // LANES):
                pick[at, k * LANES:(k + 1) * LANES] = one_hot(iota(square, 1) + k * LANES == column)

    side = []

    def deliver(h):
        yield from chain(h, 2, bk, bkx)
        size = bk.shape[2]
        for i in range(bk.shape[1]):
            root_out[i * size:(i + 1) * size, h * C:(h + 1) * C] = bkx[h, 0, i] + bk[h, i] + bkx[h, 1, i]

    def program(h):
        lanes = slice(h * C, (h + 1) * C)
        if h == 0:
            pl.semaphore_wait(barrier, nb + 1)
            loads[0].wait()

        def produce1(j, start, length):
            tm, count = tiles(length, 256)
            keep_right(h, slice(0, cols_b), crhs_ref[j, :, lanes])

            def store(i, value):
                part[h, j, pl.ds(pl.multiple_of(start + i * tm, tm), tm)] = value

            times(lambda i: ci[j, pl.ds(pl.multiple_of(start + i * tm, tm), tm), :], count, store, h, cols_b)

        yield from all_reduce(h, 0, fc, produce1)
        if h == 0:
            loads[1].wait()
        for j in range(2):
            keep_right(h, slice(0, cols_a), fc[h, j])

            def store(i, value, j=j):
                up[h, j] = value

            times(lambda i, j=j: cu[j], 1, store, h, cols_a)
        flush(h)
        yield from chain(h, 0, up, upx)
        for j in range(2):
            keep_right(h, slice(j * nl, (j + 1) * nl), upx[h, 0, j] + up[h, j] + upx[h, 1, j])

        def store_packed(at, value):
            pk1[h, at] = value

        moved(pack, store_packed, h, 2 * nl)
        yield from exchange(h, 0, pk1, rv1)
        keep_right(h, slice(0, slots), rv1[h])

        def store_rest(at, value):
            keep_right(h, at, rrhs_ref[at, lanes] - value, rhs_x)

        moved(spread, store_rest, h, slots)
        if h == 0:
            loads[2].wait()
        per = rows_a // 2

        def produce4(f, start, length):
            tm, count = tiles(length, 256)

            def store(i, value):
                part[h, f, pl.ds(pl.multiple_of(start + i * tm, tm), tm)] = value

            times(lambda i: ri[pl.ds(pl.multiple_of(f * per + start + i * tm, tm), tm), :], count, store, h, own, rhs_x)

        yield from all_reduce(h, 1, fr, produce4)
        pieces, size = bk.shape[1], bk.shape[2]
        width = min(256, own)
        kt5, _ = tiles(per, 512)
        halves = per // kt5

        keep_transposed(h, rows_a, kt5, lambda k: fr[h, k // halves, (k % halves) * kt5:(k % halves + 1) * kt5])

        for i in range(own // width):
            value = transposed_tile(
                lambda k: ri[k * kt5:(k + 1) * kt5, i * width:(i + 1) * width], rows_a, kt5, width, h
            )
            for n in range(width // size):
                bk[h, i * (width // size) + n] = value[n * size:(n + 1) * size]
            keep_right(h, slice(i * width, (i + 1) * width), value)
        flush(h)

        def store_picked(at, value):
            pk2[h, at] = value

        moved(pick, store_picked, h, own)
        if LATE[h] == 0:
            side.append((h, deliver(h)))
        yield from exchange(h, 1, pk2, rv2)
        keep_right(h, slice(0, slots), rv2[h])

        for j in range(2):
            both = dot(place[j * nl:(j + 1) * nl], rhs_w[h, :slots])
            fe[h, j] = both[:, :C] + both[:, C:]
        yield from chain(h, 1, fe, fex)
        if LATE[h] == 1:
            side.append((h, deliver(h)))

        def produce7(j, start, length):
            w7, count7 = tiles(length, 256)
            keep_transposed(h, nl, nl, lambda k: fex[h, 0, j] + fe[h, j] + fex[h, 1, j])

            def body(i, carry):
                at = pl.ds(pl.multiple_of(start + i * w7, w7), w7)
                part[h, j, at] = transposed_tile(lambda k: cu[j, :, at], nl, nl, w7, h)
                return carry

            lax.fori_loop(0, count7, body, 0)

        yield from all_reduce(h, 2, cp, produce7)
        pieces8, size8 = cb.shape[1], cb.shape[2]
        w8, count8 = tiles(cols_b, 256)
        kt8, _ = tiles(cols_a, 512)

        def produce8(n):
            j, i = n // count8, n % count8
            if i == 0:
                keep_transposed(
                    h, cols_a, kt8,
                    lambda k: fc[h, j, k * kt8:(k + 1) * kt8] - cp[h, j, k * kt8:(k + 1) * kt8],
                )
            value = transposed_tile(
                lambda k: ci[j, k * kt8:(k + 1) * kt8, i * w8:(i + 1) * w8], cols_a, kt8, w8, h
            )
            for m in range(w8 // size8):
                cb[h, n * (w8 // size8) + m] = value[m * size8:(m + 1) * size8]

        yield from chain(h, 3, cb, cbx, produce8, w8 // size8)
        for i in range(pieces8):
            j, k = i // (pieces8 // 2), i % (pieces8 // 2)
            child_out[j, k * size8:(k + 1) * size8, lanes] = cbx[h, 0, i] + cb[h, i] + cbx[h, 1, i]

    running = [program(h) for h in range(CHUNKS)]
    turn = 0

    def advance(thread):
        try:
            next(thread)
            return True
        except StopIteration:
            return False

    while any(p is not None for p in running) or side:
        for h in range(CHUNKS):
            if running[h] is not None and turn >= h * OFFSET:
                if not advance(running[h]):
                    running[h] = None
                if turn == 0:
                    route()
            for item in list(side):
                if item[0] == h and turn % GAP == h % GAP and not advance(item[1]):
                    side.remove(item)
        turn += 1
    for h in range(CHUNKS):
        flush(h)


def hand_over(root_in, child_in, root_out, child_out, root_held, child_held, sems):
    loads, stores = [], []
    for k, (src, held, dst) in enumerate(((root_in, root_held, root_out), (child_in, child_held, child_out))):
        axis = len(src.shape) - 2
        size = src.shape[axis] // COPIES
        for i in range(COPIES):
            at = (slice(None),) * axis + (pl.ds(i * size, size),)
            loads.append(pltpu.make_async_copy(src.at[at], held.at[at], sems.at[0, k, i]))
            stores.append(pltpu.make_async_copy(held.at[at], dst.at[at], sems.at[1, k, i]))
    for load in loads:
        load.start()
    for load, store in zip(loads, stores):
        load.wait()
        store.start()
    for store in stores:
        store.wait()


def per_device(nb, nr, child_inverse, child_rhs, child_update, targets, root_inverse, root_rhs):
    bits = nb.bit_length() - 1
    _, cols_a, cols_b = child_inverse.shape
    nl = child_update.shape[1]
    rows_a, own = root_inverse.shape
    R = root_rhs.shape[1]
    H, C = CHUNKS, R // CHUNKS
    cap = 2 * nl // nb
    assert rows_a == 2 * cols_a and nl == LANES
    slots = 2 * nb * cap
    root_pieces = min(PIECES, own // 32)
    child_pieces = 2 * min(PIECES // 2, cols_b // 32)
    most = max(root_pieces, child_pieces, 2)
    any_, vmem = pl.BlockSpec(memory_space=pl.ANY), pl.BlockSpec(memory_space=pltpu.VMEM)

    def sums(*dims):
        return pltpu.VMEM((H, 2, *dims, C), f32)

    def chains(pieces, rows):
        return [pltpu.VMEM((H, pieces, rows, C), f32), pltpu.VMEM((H, 4, pieces, rows, C), f32)]

    results = pl.pallas_call(
        functools.partial(kernel, nb, nr, (cols_a, cols_b, own, rows_a, nl, cap)),
        out_shape=(
            jax.ShapeDtypeStruct(root_rhs.shape, f32),
            jax.ShapeDtypeStruct(child_rhs.shape, f32),
        ),
        in_specs=[any_, vmem, any_, vmem, any_, vmem],
        out_specs=(vmem, vmem),
        scratch_shapes=[
            pltpu.VMEM(child_inverse.shape, f32),
            pltpu.VMEM(child_update.shape, f32),
            pltpu.VMEM(root_inverse.shape, f32),
            sums(cols_a),
            sums(cols_a // 2),
            sums(cols_a // 2),
            sums(cols_a),
            sums(rows_a // 2),
            sums(cols_a),
            *chains(2, nl),
            *chains(2, nl),
            *chains(root_pieces, own // root_pieces),
            *chains(child_pieces, 2 * cols_b // child_pieces),
            *[pltpu.VMEM((H, slots, C), f32)] * 4,
            pltpu.VMEM((LANES, LANES), f32),
            pltpu.VMEM((slots, 2 * nl), bf16),
            pltpu.VMEM((2 * nl, slots), bf16),
            pltpu.VMEM((own, slots), bf16),
            pltpu.VMEM((slots, own), bf16),
            pltpu.VMEM((H, max(own, cols_a, cols_b, slots), 2 * C), bf16),
            pltpu.VMEM((H, own, 2 * C), bf16),
            pltpu.VMEM((H, 2 * C, max(rows_a, cols_a, nl)), bf16),
            pltpu.SemaphoreType.DMA((3,)),
            pltpu.SemaphoreType.DMA((H, 3, 2, 2 * bits)),
            pltpu.SemaphoreType.DMA((H, 3, 2, 2 * bits)),
            pltpu.SemaphoreType.DMA((H, 2, nb)),
            pltpu.SemaphoreType.DMA((H, 2, nb)),
            pltpu.SemaphoreType.DMA((H, 4, 2, most)),
            pltpu.SemaphoreType.DMA((H, 4, 2, most)),
        ],
        compiler_params=pltpu.CompilerParams(
            collective_id=0, has_side_effects=True, vmem_limit_bytes=62 * 1024 * 1024
        ),
    )(child_inverse, child_rhs, child_update, targets, root_inverse, root_rhs)
    if COPIES == 0:
        return results
    return pl.pallas_call(
        hand_over,
        out_shape=tuple(jax.ShapeDtypeStruct(r.shape, f32) for r in results),
        in_specs=[any_, any_],
        out_specs=(any_, any_),
        scratch_shapes=[
            *[pltpu.VMEM(r.shape, f32) for r in results],
            pltpu.SemaphoreType.DMA((2, 2, COPIES)),
        ],
    )(*results)


def solution(mesh):
    return jax.shard_map(
        functools.partial(per_device, mesh.shape["bulk"], mesh.shape["row"]),
        mesh=mesh,
        in_specs=(
            P(None, "row", "bulk"),
            P(None, "bulk", None),
            P(None, "bulk", "row"),
            P(),
            P("row", "bulk"),
            P("bulk", None),
        ),
        out_specs=(P("bulk", None), P(None, "bulk", None)),
        check_vma=False,
    )
```

```python
import functools

import jax
import jax.numpy as jnp
from jax import lax
from jax.experimental import pallas as pl
from jax.experimental.pallas import tpu as pltpu
from jax.sharding import PartitionSpec as P

MESH = pl.DeviceIdType.MESH
CHUNKS = 2
OFFSET = 2
LATE = (1, 1)
GAP = 1
COPIES = 4
PASSES = 3
TM = 512
PIECES = 4
LANES = 128
f32, bf16, i32 = jnp.float32, jnp.bfloat16, jnp.int32


def split(x):
    high = x.astype(bf16)
    return high, (x - high.astype(f32)).astype(bf16)


def dot(a, b):
    return jnp.dot(a, b, preferred_element_type=f32)


def iota(shape, axis):
    return lax.broadcasted_iota(i32, shape, axis)


def one_hot(hit):
    return jnp.where(hit, 1.0, 0.0).astype(bf16)


def log2(n):
    assert n & (n - 1) == 0
    return n.bit_length() - 1


def kernel(
    nb, nr, dims,
    ci_hbm, crhs_hbm, cu_hbm, targets_ref, ri_hbm, rrhs_hbm,
    root_out, child_out,
    ci, cu, ri, crhs_ref, rrhs_ref,
    part, pair, add_r, fc, fr, cp,
    up, upx, fe, fex, bk, bkx, cb, cbx,
    pk1, rv1, pk2, rv2,
    ids, pack, place, spread, pick,
    rhs_w, rhs_x, tmp_t,
    load_sem, ar_s, ar_r, a2a_s, a2a_r, ch_s, ch_r,
):
    bits = log2(nb)
    me = lax.axis_index("bulk")
    row = lax.axis_index("row")
    C = fc.shape[-1]
    cols_a, cols_b, own, rows_a, nl, cap = dims
    orders = (list(range(1, bits)), list(range(1, bits))[::-1])

    loads = [
        pltpu.make_async_copy(ci_hbm, ci, load_sem.at[0]),
        pltpu.make_async_copy(cu_hbm, cu, load_sem.at[1]),
        pltpu.make_async_copy(ri_hbm, ri, load_sem.at[2]),
        pltpu.make_async_copy(crhs_hbm, crhs_ref, load_sem.at[3]),
        pltpu.make_async_copy(rrhs_hbm, rrhs_ref, load_sem.at[4]),
    ]
    loads[3].start()
    loads[0].start()

    def bit_of(bit):
        return (me // (1 << bit)) % 2

    def across(bit):
        return me + (1 << bit) * (1 - 2 * bit_of(bit))

    right = lax.rem(row + 1, nr)
    left = lax.rem(row + nr - 1, nr)
    barrier = pltpu.get_barrier_semaphore()
    for d in range(1, nb):
        pl.semaphore_signal(barrier, inc=1, device_id={"bulk": lax.rem(me + d, nb)}, device_id_type=MESH)
    for side in (left, right):
        pl.semaphore_signal(barrier, inc=1, device_id={"row": side}, device_id_type=MESH)

    def remote(src, dst, send, recv, **where):
        return pltpu.make_async_remote_copy(
            src_ref=src, dst_ref=dst, send_sem=send, recv_sem=recv, device_id=where, device_id_type=MESH
        )

    for x in (upx, fex, bkx, cbx):
        for end, where in enumerate((0, nr - 1)):
            @pl.when(row == where)
            def _():
                for h in range(CHUNKS):
                    x[h, end] = jnp.zeros(x.shape[2:], f32)

    pending = [[] for _ in range(CHUNKS)]

    def flush(h):
        for finish in pending[h]:
            finish()
        pending[h] = []

    def all_reduce(h, which, out, produce):
        half = part.shape[2] // 2
        mine = pl.multiple_of((me % 2) * half, half)
        theirs = pl.multiple_of((1 - me % 2) * half, half)
        sends = []

        def send(f, step, src, dst, bit):
            copy = remote(src, dst, ar_s.at[h, which, f, step], ar_r.at[h, which, f, step], bulk=across(bit))
            copy.start()
            sends.append(copy.wait_send)
            return copy

        def rows(start, length):
            return pl.ds(pl.multiple_of(start, length), length)

        flush(h)
        pairs = []
        for f in range(2):
            produce(f, theirs, half)
            pairs.append(send(f, 0, part.at[h, f, pl.ds(theirs, half)], pair.at[h, f], 0))
        starts, flights, length, off = [mine, mine], [None, None], half, 0

        def halve(f, step):
            n, bit = length // 2, bit_of(orders[f][step])
            flights[f] = send(
                f, 1 + step, part.at[h, f, rows(starts[f] + (1 - bit) * n, n)], add_r.at[h, f, pl.ds(off, n)],
                orders[f][step],
            )
            starts[f] = starts[f] + bit * n

        for f in range(2):
            produce(f, mine, half)
            pairs[f].wait_recv()
            part[h, f, pl.ds(mine, half)] += pair[h, f]
            halve(f, 0)
        yield
        for step in range(bits - 1):
            length //= 2
            for f in range(2):
                flights[f].wait_recv()
                at = rows(starts[f], length)
                total = part[h, f, at] + add_r[h, f, pl.ds(off, length)]
                if step < bits - 2:
                    part[h, f, at] = total
                    off += length
                    halve(f, step + 1)
                    off -= length
                else:
                    out[h, f, at] = total
                    at = out.at[h, f, at]
                    flights[f] = send(f, bits, at, at, orders[f][step])
            off += length
            yield
        for step in reversed(range(bits - 1)):
            for f in range(2):
                flights[f].wait_recv()
                starts[f] = starts[f] - bit_of(orders[f][step]) * length
                at = out.at[h, f, rows(starts[f], 2 * length)]
                to = orders[f][step - 1] if step > 0 else 0
                flights[f] = send(f, 2 * bits - 1 - step, at, at, to)
            length *= 2
            yield
        for f in range(2):
            flights[f].wait_recv()
        pending[h] += sends

    def exchange(h, which, packed, arrived):
        n = 2 * cap
        here = pl.ds(pl.multiple_of(me * n, n), n)
        copies = []
        for d in range(1, nb):
            peer = lax.rem(me + d, nb)
            copy = remote(
                packed.at[h, pl.ds(pl.multiple_of(peer * n, n), n)], arrived.at[h, here],
                a2a_s.at[h, which, d], a2a_r.at[h, which, d], bulk=peer,
            )
            copy.start()
            copies.append(copy)
        arrived[h, here] = packed[h, here]
        yield
        for copy in copies:
            copy.wait_recv()
        pending[h] += [copy.wait_send for copy in copies]

    def chain(h, which, p, x, produce=None, stride=1):
        pieces = p.shape[1]

        def flow(side, i, has_source, has_target, target):
            copy = remote(
                x.at[h, 2 + side, i], x.at[h, side, i],
                ch_s.at[h, which, side, i], ch_r.at[h, which, side, i], row=target,
            )

            @pl.when(has_source)
            def _():
                copy.wait_recv()

            @pl.when(has_target)
            def _():
                x[h, 2 + side, i] = x[h, side, i] + p[h, i]
                copy.start()

        for t in range(pieces + nr - 1):
            if t > 0:
                yield
            if produce is not None and t < pieces and t % stride == 0:
                produce(t // stride)
            i = t - row

            @pl.when((i >= 0) & (i < pieces))
            def _():
                flow(0, i, row > 0, row < nr - 1, right)

            k = t - (nr - 1 - row)

            @pl.when((k >= 0) & (k < pieces))
            def _():
                flow(1, k, row < nr - 1, row > 0, left)

        def finish():
            for i in range(pieces):
                for side, has_target, target in ((0, row < nr - 1, right), (1, row > 0, left)):
                    @pl.when(has_target)
                    def _():
                        remote(
                            x.at[h, 2 + side, i], x.at[h, side, i],
                            ch_s.at[h, which, side, i], ch_r.at[h, which, side, i], row=target,
                        ).wait_send()

        pending[h].append(finish)

    def times(a_tile, count, store, h, width, w=rhs_w):
        def body(i, carry):
            high, low = split(a_tile(i))
            both = dot(high, w[h, :width])
            if PASSES == 3:
                store(i, both[:, :C] + (both[:, C:] + dot(low, w[h, :width, :C])))
            else:
                both += dot(low, w[h, :width])
                store(i, both[:, :C] + both[:, C:])
            return carry

        lax.fori_loop(0, count, body, 0)

    def moved(rows, store, h, width, tile=256):
        tile = min(tile, rows.shape[0])

        def body(i, carry):
            at = pl.ds(pl.multiple_of(i * tile, tile), tile)
            both = dot(rows[at], rhs_w[h, :width])
            store(at, both[:, :C] + both[:, C:])
            return carry

        lax.fori_loop(0, rows.shape[0] // tile, body, 0)

    def keep_right(h, at, value, w=rhs_w):
        high, low = split(value)
        w[h, at, :C] = high
        w[h, at, C:] = low

    def keep_transposed(h, depth, k_tile, y_tile):
        for k in range(depth // k_tile):
            high, low = split(y_tile(k).T)
            tmp_t[h, :C, k * k_tile:(k + 1) * k_tile] = high
            tmp_t[h, C:, k * k_tile:(k + 1) * k_tile] = low

    def transposed_tile(a_tile, depth, k_tile, width, h):
        total = jnp.zeros((2 * C, width), f32)
        extra = jnp.zeros((C, width), f32)
        for k in range(depth // k_tile):
            high, low = split(a_tile(k))
            y = tmp_t[h, :, k * k_tile:(k + 1) * k_tile]
            total += dot(y, high)
            if PASSES == 3:
                extra += dot(y[:C], low)
            else:
                total += dot(y, low)
        return (total[:C] + (total[C:] + extra)).T

    def tiles(n, most):
        size = min(n, most)
        return size, n // size

    slots = nb * 2 * cap

    def turned(line):
        return jnp.broadcast_to(line, (LANES, LANES)).T

    def route():
        square = (LANES, LANES)
        before = iota(square, 0) < iota(square, 1)
        ids[...] = jnp.full(ids.shape, -1.0, f32)
        for j in range(2):
            for b in range(nb):
                ids[j * nb + b:j * nb + b + 1, :] = targets_ref[j:j + 1, b * nl:(b + 1) * nl].astype(f32)
        for j in range(2):
            line = ids[pl.ds(j * nb + me, 1), :]
            owner = lax.shift_right_logical(line.astype(i32), log2(own)).astype(f32)
            same = (turned(owner) == owner) & before
            rank = jnp.sum(jnp.where(same, 1.0, 0.0), axis=0, keepdims=True)
            position = owner * (2.0 * cap) + (rank + j * cap)
            column = turned(position).astype(i32)
            at = slice(j * nl, (j + 1) * nl)
            pack[:, at] = one_hot(iota((slots, nl), 0) == position.astype(i32))
            for g in range(slots // LANES):
                place[at, g * LANES:(g + 1) * LANES] = one_hot(iota(square, 1) + g * LANES == column)
        first = (me * own).astype(f32)
        local = ids[...] - first
        inside = (local >= 0.0) & (local < float(own))
        ones = jnp.where(inside, 1.0, 0.0).astype(bf16)
        rank = dot(ones, one_hot(before))
        index = iota(ids.shape, 0)
        child = jnp.where(index >= nb, 1, 0)
        base = (index - nb * child) * (2 * cap) + child * cap
        position = jnp.where(inside, rank + base.astype(f32), -1.0)
        position, local = position.T, local.T
        fill = iota(square, 1).astype(f32)
        lines = []
        for g in range(slots // LANES):
            total = jnp.zeros(square, f32)
            for j in range(2):
                for b in range(nb):
                    if (b * 2 * cap + j * cap) // LANES == g:
                        r = j * nb + b
                        hit = position[:, r:r + 1] == fill + float(g * LANES)
                        total = total + jnp.where(hit, local[:, r:r + 1] + 1.0, 0.0)
            lines.append(jnp.sum(total, axis=0, keepdims=True) - 1.0)
        for g, line in enumerate(lines):
            at = slice(g * LANES, (g + 1) * LANES)
            spread[:, at] = one_hot(iota((own, LANES), 0) == line.astype(i32))
            column = turned(line).astype(i32)
            for k in range(own // LANES):
                pick[at, k * LANES:(k + 1) * LANES] = one_hot(iota(square, 1) + k * LANES == column)

    side = []

    def deliver(h):
        yield from chain(h, 2, bk, bkx)
        size = bk.shape[2]
        for i in range(bk.shape[1]):
            root_out[i * size:(i + 1) * size, h * C:(h + 1) * C] = bkx[h, 0, i] + bk[h, i] + bkx[h, 1, i]

    def program(h):
        lanes = slice(h * C, (h + 1) * C)
        if h == 0:
            pl.semaphore_wait(barrier, nb + 1)
            loads[3].wait()
            loads[0].wait()
            loads[1].start()
            loads[4].start()
            loads[2].start()

        def produce1(j, start, length):
            tm, count = tiles(length, TM)
            keep_right(h, slice(0, cols_b), crhs_ref[j, :, lanes])

            def store(i, value):
                part[h, j, pl.ds(pl.multiple_of(start + i * tm, tm), tm)] = value

            times(lambda i: ci[j, pl.ds(pl.multiple_of(start + i * tm, tm), tm), :], count, store, h, cols_b)

        yield from all_reduce(h, 0, fc, produce1)
        if h == 0:
            loads[1].wait()
            loads[4].wait()
        for j in range(2):
            keep_right(h, slice(0, cols_a), fc[h, j])

            def store(i, value, j=j):
                up[h, j] = value

            times(lambda i, j=j: cu[j], 1, store, h, cols_a)
        flush(h)
        yield from chain(h, 0, up, upx)
        for j in range(2):
            keep_right(h, slice(j * nl, (j + 1) * nl), upx[h, 0, j] + up[h, j] + upx[h, 1, j])

        def store_packed(at, value):
            pk1[h, at] = value

        moved(pack, store_packed, h, 2 * nl)
        yield from exchange(h, 0, pk1, rv1)
        keep_right(h, slice(0, slots), rv1[h])

        def store_rest(at, value):
            keep_right(h, at, rrhs_ref[at, lanes] - value, rhs_x)

        moved(spread, store_rest, h, slots)
        if h == 0:
            loads[2].wait()
        per = rows_a // 2

        def produce4(f, start, length):
            tm, count = tiles(length, TM)

            def store(i, value):
                part[h, f, pl.ds(pl.multiple_of(start + i * tm, tm), tm)] = value

            times(lambda i: ri[pl.ds(pl.multiple_of(f * per + start + i * tm, tm), tm), :], count, store, h, own, rhs_x)

        yield from all_reduce(h, 1, fr, produce4)
        pieces, size = bk.shape[1], bk.shape[2]
        width = min(256, own)
        kt5, _ = tiles(per, 512)
        halves = per // kt5

        keep_transposed(h, rows_a, kt5, lambda k: fr[h, k // halves, (k % halves) * kt5:(k % halves + 1) * kt5])

        for i in range(own // width):
            value = transposed_tile(
                lambda k: ri[k * kt5:(k + 1) * kt5, i * width:(i + 1) * width], rows_a, kt5, width, h
            )
            for n in range(width // size):
                bk[h, i * (width // size) + n] = value[n * size:(n + 1) * size]
            keep_right(h, slice(i * width, (i + 1) * width), value)
        flush(h)

        def store_picked(at, value):
            pk2[h, at] = value

        moved(pick, store_picked, h, own)
        if LATE[h] == 0:
            side.append((h, deliver(h)))
        yield from exchange(h, 1, pk2, rv2)
        keep_right(h, slice(0, slots), rv2[h])

        for j in range(2):
            both = dot(place[j * nl:(j + 1) * nl], rhs_w[h, :slots])
            fe[h, j] = both[:, :C] + both[:, C:]
        yield from chain(h, 1, fe, fex)
        if LATE[h] == 1:
            side.append((h, deliver(h)))

        def produce7(j, start, length):
            w7, count7 = tiles(length, 256)
            keep_transposed(h, nl, nl, lambda k: fex[h, 0, j] + fe[h, j] + fex[h, 1, j])

            def body(i, carry):
                at = pl.ds(pl.multiple_of(start + i * w7, w7), w7)
                part[h, j, at] = transposed_tile(lambda k: cu[j, :, at], nl, nl, w7, h)
                return carry

            lax.fori_loop(0, count7, body, 0)

        yield from all_reduce(h, 2, cp, produce7)
        pieces8, size8 = cb.shape[1], cb.shape[2]
        w8, count8 = tiles(cols_b, 256)
        kt8, _ = tiles(cols_a, 512)

        def produce8(n):
            j, i = n // count8, n % count8
            if i == 0:
                keep_transposed(
                    h, cols_a, kt8,
                    lambda k: fc[h, j, k * kt8:(k + 1) * kt8] - cp[h, j, k * kt8:(k + 1) * kt8],
                )
            value = transposed_tile(
                lambda k: ci[j, k * kt8:(k + 1) * kt8, i * w8:(i + 1) * w8], cols_a, kt8, w8, h
            )
            for m in range(w8 // size8):
                cb[h, n * (w8 // size8) + m] = value[m * size8:(m + 1) * size8]

        yield from chain(h, 3, cb, cbx, produce8, w8 // size8)
        for i in range(pieces8):
            j, k = i // (pieces8 // 2), i % (pieces8 // 2)
            child_out[j, k * size8:(k + 1) * size8, lanes] = cbx[h, 0, i] + cb[h, i] + cbx[h, 1, i]

    running = [program(h) for h in range(CHUNKS)]
    turn = 0

    def advance(thread):
        try:
            next(thread)
            return True
        except StopIteration:
            return False

    while any(p is not None for p in running) or side:
        for h in range(CHUNKS):
            if running[h] is not None and turn >= h * OFFSET:
                if not advance(running[h]):
                    running[h] = None
                if turn == 0:
                    route()
            for item in list(side):
                if item[0] == h and turn % GAP == h % GAP and not advance(item[1]):
                    side.remove(item)
        turn += 1
    for h in range(CHUNKS):
        flush(h)


def hand_over(root_in, child_in, root_out, child_out, root_held, child_held, sems):
    loads, stores = [], []
    for k, (src, held, dst) in enumerate(((root_in, root_held, root_out), (child_in, child_held, child_out))):
        axis = len(src.shape) - 2
        size = src.shape[axis] // COPIES
        for i in range(COPIES):
            at = (slice(None),) * axis + (pl.ds(i * size, size),)
            loads.append(pltpu.make_async_copy(src.at[at], held.at[at], sems.at[0, k, i]))
            stores.append(pltpu.make_async_copy(held.at[at], dst.at[at], sems.at[1, k, i]))
    for load in loads:
        load.start()
    for load, store in zip(loads, stores):
        load.wait()
        store.start()
    for store in stores:
        store.wait()


def per_device(nb, nr, child_inverse, child_rhs, child_update, targets, root_inverse, root_rhs):
    bits = nb.bit_length() - 1
    _, cols_a, cols_b = child_inverse.shape
    nl = child_update.shape[1]
    rows_a, own = root_inverse.shape
    R = root_rhs.shape[1]
    H, C = CHUNKS, R // CHUNKS
    cap = 2 * nl // nb
    assert rows_a == 2 * cols_a and nl == LANES
    slots = 2 * nb * cap
    root_pieces = min(PIECES, own // 32)
    child_pieces = 2 * min(PIECES // 2, cols_b // 32)
    most = max(root_pieces, child_pieces, 2)
    any_, vmem = pl.BlockSpec(memory_space=pl.ANY), pl.BlockSpec(memory_space=pltpu.VMEM)

    def sums(*dims):
        return pltpu.VMEM((H, 2, *dims, C), f32)

    def chains(pieces, rows):
        return [pltpu.VMEM((H, pieces, rows, C), f32), pltpu.VMEM((H, 4, pieces, rows, C), f32)]

    results = pl.pallas_call(
        functools.partial(kernel, nb, nr, (cols_a, cols_b, own, rows_a, nl, cap)),
        out_shape=(
            jax.ShapeDtypeStruct(root_rhs.shape, f32),
            jax.ShapeDtypeStruct(child_rhs.shape, f32),
        ),
        in_specs=[any_, any_, any_, vmem, any_, any_],
        out_specs=(vmem, vmem),
        scratch_shapes=[
            pltpu.VMEM(child_inverse.shape, f32),
            pltpu.VMEM(child_update.shape, f32),
            pltpu.VMEM(root_inverse.shape, f32),
            pltpu.VMEM(child_rhs.shape, f32),
            pltpu.VMEM(root_rhs.shape, f32),
            sums(cols_a),
            sums(cols_a // 2),
            sums(cols_a // 2),
            sums(cols_a),
            sums(rows_a // 2),
            sums(cols_a),
            *chains(2, nl),
            *chains(2, nl),
            *chains(root_pieces, own // root_pieces),
            *chains(child_pieces, 2 * cols_b // child_pieces),
            *[pltpu.VMEM((H, slots, C), f32)] * 4,
            pltpu.VMEM((LANES, LANES), f32),
            pltpu.VMEM((slots, 2 * nl), bf16),
            pltpu.VMEM((2 * nl, slots), bf16),
            pltpu.VMEM((own, slots), bf16),
            pltpu.VMEM((slots, own), bf16),
            pltpu.VMEM((H, max(own, cols_a, cols_b, slots), 2 * C), bf16),
            pltpu.VMEM((H, own, 2 * C), bf16),
            pltpu.VMEM((H, 2 * C, max(rows_a, cols_a, nl)), bf16),
            pltpu.SemaphoreType.DMA((5,)),
            pltpu.SemaphoreType.DMA((H, 3, 2, 2 * bits)),
            pltpu.SemaphoreType.DMA((H, 3, 2, 2 * bits)),
            pltpu.SemaphoreType.DMA((H, 2, nb)),
            pltpu.SemaphoreType.DMA((H, 2, nb)),
            pltpu.SemaphoreType.DMA((H, 4, 2, most)),
            pltpu.SemaphoreType.DMA((H, 4, 2, most)),
        ],
        compiler_params=pltpu.CompilerParams(
            collective_id=0, has_side_effects=True, vmem_limit_bytes=62 * 1024 * 1024
        ),
    )(child_inverse, child_rhs, child_update, targets, root_inverse, root_rhs)
    if COPIES == 0:
        return results
    return pl.pallas_call(
        hand_over,
        out_shape=tuple(jax.ShapeDtypeStruct(r.shape, f32) for r in results),
        in_specs=[any_, any_],
        out_specs=(any_, any_),
        scratch_shapes=[
            *[pltpu.VMEM(r.shape, f32) for r in results],
            pltpu.SemaphoreType.DMA((2, 2, COPIES)),
        ],
    )(*results)


def solution(mesh):
    return jax.shard_map(
        functools.partial(per_device, mesh.shape["bulk"], mesh.shape["row"]),
        mesh=mesh,
        in_specs=(
            P(None, "row", "bulk"),
            P(None, "bulk", None),
            P(None, "bulk", "row"),
            P(),
            P("row", "bulk"),
            P("bulk", None),
        ),
        out_specs=(P("bulk", None), P(None, "bulk", None)),
        check_vma=False,
    )
```

```python
import functools

import jax
import jax.numpy as jnp
from jax import lax
from jax.experimental import pallas as pl
from jax.experimental.pallas import tpu as pltpu
from jax.sharding import PartitionSpec as P

MESH = pl.DeviceIdType.MESH
CHUNKS = 2
OFFSET = 1
LATE = (1, 1)
GAP = 1
COPIES = 4
PASSES = 3
SMALL = 1
TM = 512
PIECES = 4
LANES = 128
f32, bf16, i32 = jnp.float32, jnp.bfloat16, jnp.int32


def split(x):
    high = x.astype(bf16)
    return high, (x - high.astype(f32)).astype(bf16)


def dot(a, b):
    return jnp.dot(a, b, preferred_element_type=f32)


def iota(shape, axis):
    return lax.broadcasted_iota(i32, shape, axis)


def one_hot(hit):
    return jnp.where(hit, 1.0, 0.0).astype(bf16)


def log2(n):
    assert n & (n - 1) == 0
    return n.bit_length() - 1


def kernel(
    nb, nr, dims,
    ci_hbm, crhs_hbm, cu_hbm, targets_ref, ri_hbm, rrhs_hbm,
    root_out, child_out,
    ci, cu, ri, crhs_ref, rrhs_ref,
    part, pair, add_r, fc, fr, cp,
    up, upx, fe, fex, bk, bkx, cb, cbx,
    pk1, rv1, pk2, rv2,
    ids, pack, place, spread, pick,
    rhs_w, rhs_x, tmp_t,
    load_sem, ar_s, ar_r, a2a_s, a2a_r, ch_s, ch_r,
):
    bits = log2(nb)
    me = lax.axis_index("bulk")
    row = lax.axis_index("row")
    C = fc.shape[-1]
    cols_a, cols_b, own, rows_a, nl, cap = dims
    orders = (list(range(1, bits)), list(range(1, bits))[::-1])

    loads = [
        pltpu.make_async_copy(ci_hbm, ci, load_sem.at[0]),
        pltpu.make_async_copy(cu_hbm, cu, load_sem.at[1]),
        pltpu.make_async_copy(ri_hbm, ri, load_sem.at[2]),
        pltpu.make_async_copy(crhs_hbm, crhs_ref, load_sem.at[3]),
        pltpu.make_async_copy(rrhs_hbm, rrhs_ref, load_sem.at[4]),
    ]
    loads[3].start()
    loads[0].start()

    def bit_of(bit):
        return (me // (1 << bit)) % 2

    def across(bit):
        return me + (1 << bit) * (1 - 2 * bit_of(bit))

    right = lax.rem(row + 1, nr)
    left = lax.rem(row + nr - 1, nr)
    barrier = pltpu.get_barrier_semaphore()
    for d in range(1, nb):
        pl.semaphore_signal(barrier, inc=1, device_id={"bulk": lax.rem(me + d, nb)}, device_id_type=MESH)
    for side in (left, right):
        pl.semaphore_signal(barrier, inc=1, device_id={"row": side}, device_id_type=MESH)

    def remote(src, dst, send, recv, **where):
        return pltpu.make_async_remote_copy(
            src_ref=src, dst_ref=dst, send_sem=send, recv_sem=recv, device_id=where, device_id_type=MESH
        )

    for x in (upx, fex, bkx, cbx):
        for end, where in enumerate((0, nr - 1)):
            @pl.when(row == where)
            def _():
                for h in range(CHUNKS):
                    x[h, end] = jnp.zeros(x.shape[2:], f32)

    pending = [[] for _ in range(CHUNKS)]

    def flush(h):
        for finish in pending[h]:
            finish()
        pending[h] = []

    def all_reduce(h, which, out, produce):
        half = part.shape[2] // 2
        mine = pl.multiple_of((me % 2) * half, half)
        theirs = pl.multiple_of((1 - me % 2) * half, half)
        sends = []

        def send(f, step, src, dst, bit):
            copy = remote(src, dst, ar_s.at[h, which, f, step], ar_r.at[h, which, f, step], bulk=across(bit))
            copy.start()
            sends.append(copy.wait_send)
            return copy

        def rows(start, length):
            return pl.ds(pl.multiple_of(start, length), length)

        flush(h)
        pairs = []
        for f in range(2):
            produce(f, theirs, half)
            pairs.append(send(f, 0, part.at[h, f, pl.ds(theirs, half)], pair.at[h, f], 0))
        starts, flights, length, off = [mine, mine], [None, None], half, 0

        def halve(f, step):
            n, bit = length // 2, bit_of(orders[f][step])
            flights[f] = send(
                f, 1 + step, part.at[h, f, rows(starts[f] + (1 - bit) * n, n)], add_r.at[h, f, pl.ds(off, n)],
                orders[f][step],
            )
            starts[f] = starts[f] + bit * n

        for f in range(2):
            produce(f, mine, half)
            pairs[f].wait_recv()
            part[h, f, pl.ds(mine, half)] += pair[h, f]
            halve(f, 0)
        yield
        for step in range(bits - 1):
            length //= 2
            for f in range(2):
                flights[f].wait_recv()
                at = rows(starts[f], length)
                total = part[h, f, at] + add_r[h, f, pl.ds(off, length)]
                if step < bits - 2:
                    part[h, f, at] = total
                    off += length
                    halve(f, step + 1)
                    off -= length
                else:
                    out[h, f, at] = total
                    at = out.at[h, f, at]
                    flights[f] = send(f, bits, at, at, orders[f][step])
            off += length
            yield
        for step in reversed(range(bits - 1)):
            for f in range(2):
                flights[f].wait_recv()
                starts[f] = starts[f] - bit_of(orders[f][step]) * length
                at = out.at[h, f, rows(starts[f], 2 * length)]
                to = orders[f][step - 1] if step > 0 else 0
                flights[f] = send(f, 2 * bits - 1 - step, at, at, to)
            length *= 2
            yield
        for f in range(2):
            flights[f].wait_recv()
        pending[h] += sends

    def exchange(h, which, packed, arrived):
        n = 2 * cap
        here = pl.ds(pl.multiple_of(me * n, n), n)
        copies = []
        for d in range(1, nb):
            peer = lax.rem(me + d, nb)
            copy = remote(
                packed.at[h, pl.ds(pl.multiple_of(peer * n, n), n)], arrived.at[h, here],
                a2a_s.at[h, which, d], a2a_r.at[h, which, d], bulk=peer,
            )
            copy.start()
            copies.append(copy)
        arrived[h, here] = packed[h, here]
        yield
        for copy in copies:
            copy.wait_recv()
        pending[h] += [copy.wait_send for copy in copies]

    def chain(h, which, p, x, produce=None, stride=1):
        pieces = p.shape[1]

        def flow(side, i, has_source, has_target, target):
            copy = remote(
                x.at[h, 2 + side, i], x.at[h, side, i],
                ch_s.at[h, which, side, i], ch_r.at[h, which, side, i], row=target,
            )

            @pl.when(has_source)
            def _():
                copy.wait_recv()

            @pl.when(has_target)
            def _():
                x[h, 2 + side, i] = x[h, side, i] + p[h, i]
                copy.start()

        for t in range(pieces + nr - 1):
            if t > 0:
                yield
            if produce is not None and t < pieces and t % stride == 0:
                produce(t // stride)
            i = t - row

            @pl.when((i >= 0) & (i < pieces))
            def _():
                flow(0, i, row > 0, row < nr - 1, right)

            k = t - (nr - 1 - row)

            @pl.when((k >= 0) & (k < pieces))
            def _():
                flow(1, k, row < nr - 1, row > 0, left)

        def finish():
            for i in range(pieces):
                for side, has_target, target in ((0, row < nr - 1, right), (1, row > 0, left)):
                    @pl.when(has_target)
                    def _():
                        remote(
                            x.at[h, 2 + side, i], x.at[h, side, i],
                            ch_s.at[h, which, side, i], ch_r.at[h, which, side, i], row=target,
                        ).wait_send()

        pending[h].append(finish)

    def times(a_tile, count, store, h, width, w=rhs_w):
        def body(i, carry):
            high, low = split(a_tile(i))
            both = dot(high, w[h, :width])
            if PASSES == 3:
                store(i, both[:, :C] + (both[:, C:] + dot(low, w[h, :width, :C])))
            else:
                both += dot(low, w[h, :width])
                store(i, both[:, :C] + both[:, C:])
            return carry

        lax.fori_loop(0, count, body, 0)

    def moved(rows, store, h, width, tile=256):
        tile = min(tile, rows.shape[0])

        def body(i, carry):
            at = pl.ds(pl.multiple_of(i * tile, tile), tile)
            both = dot(rows[at], rhs_w[h, :width])
            store(at, both[:, :C] + both[:, C:])
            return carry

        lax.fori_loop(0, rows.shape[0] // tile, body, 0)

    def keep_right(h, at, value, w=rhs_w):
        high, low = split(value)
        w[h, at, :C] = high
        w[h, at, C:] = low

    def keep_transposed(h, depth, k_tile, y_tile):
        for k in range(depth // k_tile):
            high, low = split(y_tile(k).T)
            tmp_t[h, :C, k * k_tile:(k + 1) * k_tile] = high
            tmp_t[h, C:, k * k_tile:(k + 1) * k_tile] = low

    def transposed_tile(a_tile, depth, k_tile, width, h):
        total = jnp.zeros((2 * C, width), f32)
        extra = jnp.zeros((C, width), f32)
        for k in range(depth // k_tile):
            high, low = split(a_tile(k))
            y = tmp_t[h, :, k * k_tile:(k + 1) * k_tile]
            total += dot(y, high)
            if PASSES == 3:
                extra += dot(y[:C], low)
            else:
                total += dot(y, low)
        return (total[:C] + (total[C:] + extra)).T

    def tiles(n, most):
        size = min(n, most)
        return size, n // size

    slots = nb * 2 * cap

    def turned(line):
        return jnp.broadcast_to(line, (LANES, LANES)).T

    def route():
        square = (LANES, LANES)
        before = iota(square, 0) < iota(square, 1)
        ids[...] = jnp.full(ids.shape, -1.0, f32)
        for j in range(2):
            for b in range(nb):
                ids[j * nb + b:j * nb + b + 1, :] = targets_ref[j:j + 1, b * nl:(b + 1) * nl].astype(f32)
        for j in range(2):
            line = ids[pl.ds(j * nb + me, 1), :]
            owner = lax.shift_right_logical(line.astype(i32), log2(own)).astype(f32)
            same = (turned(owner) == owner) & before
            rank = jnp.sum(jnp.where(same, 1.0, 0.0), axis=0, keepdims=True)
            position = owner * (2.0 * cap) + (rank + j * cap)
            column = turned(position).astype(i32)
            at = slice(j * nl, (j + 1) * nl)
            pack[:, at] = one_hot(iota((slots, nl), 0) == position.astype(i32))
            for g in range(slots // LANES):
                place[at, g * LANES:(g + 1) * LANES] = one_hot(iota(square, 1) + g * LANES == column)
        first = (me * own).astype(f32)
        local = ids[...] - first
        inside = (local >= 0.0) & (local < float(own))
        ones = jnp.where(inside, 1.0, 0.0).astype(bf16)
        rank = dot(ones, one_hot(before))
        index = iota(ids.shape, 0)
        child = jnp.where(index >= nb, 1, 0)
        base = (index - nb * child) * (2 * cap) + child * cap
        position = jnp.where(inside, rank + base.astype(f32), -1.0)
        position, local = position.T, local.T
        fill = iota(square, 1).astype(f32)
        lines = []
        for g in range(slots // LANES):
            total = jnp.zeros(square, f32)
            for j in range(2):
                for b in range(nb):
                    if (b * 2 * cap + j * cap) // LANES == g:
                        r = j * nb + b
                        hit = position[:, r:r + 1] == fill + float(g * LANES)
                        total = total + jnp.where(hit, local[:, r:r + 1] + 1.0, 0.0)
            lines.append(jnp.sum(total, axis=0, keepdims=True) - 1.0)
        for g, line in enumerate(lines):
            at = slice(g * LANES, (g + 1) * LANES)
            spread[:, at] = one_hot(iota((own, LANES), 0) == line.astype(i32))
            column = turned(line).astype(i32)
            for k in range(own // LANES):
                pick[at, k * LANES:(k + 1) * LANES] = one_hot(iota(square, 1) + k * LANES == column)

    def seat(j):
        if SMALL == 1:
            return 0, slice(j * nl, (j + 1) * nl)
        return j, slice(0, nl)

    side = []

    def deliver(h):
        yield from chain(h, 2, bk, bkx)
        size = bk.shape[2]
        for i in range(bk.shape[1]):
            root_out[i * size:(i + 1) * size, h * C:(h + 1) * C] = bkx[h, 0, i] + bk[h, i] + bkx[h, 1, i]

    def program(h):
        lanes = slice(h * C, (h + 1) * C)
        if h == 0:
            pl.semaphore_wait(barrier, nb + 1)
            loads[3].wait()
            loads[0].wait()
            loads[1].start()
            loads[4].start()
            loads[2].start()

        def produce1(j, start, length):
            tm, count = tiles(length, TM)
            keep_right(h, slice(0, cols_b), crhs_ref[j, :, lanes])

            def store(i, value):
                part[h, j, pl.ds(pl.multiple_of(start + i * tm, tm), tm)] = value

            times(lambda i: ci[j, pl.ds(pl.multiple_of(start + i * tm, tm), tm), :], count, store, h, cols_b)

        yield from all_reduce(h, 0, fc, produce1)
        if h == 0:
            loads[1].wait()
            loads[4].wait()
        for j in range(2):
            keep_right(h, slice(0, cols_a), fc[h, j])

            def store(i, value, j=j):
                up[(h, *seat(j))] = value

            times(lambda i, j=j: cu[j], 1, store, h, cols_a)
        flush(h)
        yield from chain(h, 0, up, upx)
        for j in range(2):
            keep_right(h, slice(j * nl, (j + 1) * nl), upx[(h, 0, *seat(j))] + up[(h, *seat(j))] + upx[(h, 1, *seat(j))])

        def store_packed(at, value):
            pk1[h, at] = value

        moved(pack, store_packed, h, 2 * nl)
        yield from exchange(h, 0, pk1, rv1)
        keep_right(h, slice(0, slots), rv1[h])

        def store_rest(at, value):
            keep_right(h, at, rrhs_ref[at, lanes] - value, rhs_x)

        moved(spread, store_rest, h, slots)
        if h == 0:
            loads[2].wait()
        per = rows_a // 2

        def produce4(f, start, length):
            tm, count = tiles(length, TM)

            def store(i, value):
                part[h, f, pl.ds(pl.multiple_of(start + i * tm, tm), tm)] = value

            times(lambda i: ri[pl.ds(pl.multiple_of(f * per + start + i * tm, tm), tm), :], count, store, h, own, rhs_x)

        yield from all_reduce(h, 1, fr, produce4)
        pieces, size = bk.shape[1], bk.shape[2]
        width = min(256, own)
        kt5, _ = tiles(per, 512)
        halves = per // kt5

        keep_transposed(h, rows_a, kt5, lambda k: fr[h, k // halves, (k % halves) * kt5:(k % halves + 1) * kt5])

        for i in range(own // width):
            value = transposed_tile(
                lambda k: ri[k * kt5:(k + 1) * kt5, i * width:(i + 1) * width], rows_a, kt5, width, h
            )
            for n in range(width // size):
                bk[h, i * (width // size) + n] = value[n * size:(n + 1) * size]
            keep_right(h, slice(i * width, (i + 1) * width), value)
        flush(h)

        def store_picked(at, value):
            pk2[h, at] = value

        moved(pick, store_picked, h, own)
        if LATE[h] == 0:
            side.append((h, deliver(h)))
        yield from exchange(h, 1, pk2, rv2)
        keep_right(h, slice(0, slots), rv2[h])

        for j in range(2):
            both = dot(place[j * nl:(j + 1) * nl], rhs_w[h, :slots])
            fe[(h, *seat(j))] = both[:, :C] + both[:, C:]
        yield from chain(h, 1, fe, fex)
        if LATE[h] == 1:
            side.append((h, deliver(h)))

        def produce7(j, start, length):
            w7, count7 = tiles(length, 256)
            keep_transposed(h, nl, nl, lambda k: fex[(h, 0, *seat(j))] + fe[(h, *seat(j))] + fex[(h, 1, *seat(j))])

            def body(i, carry):
                at = pl.ds(pl.multiple_of(start + i * w7, w7), w7)
                part[h, j, at] = transposed_tile(lambda k: cu[j, :, at], nl, nl, w7, h)
                return carry

            lax.fori_loop(0, count7, body, 0)

        yield from all_reduce(h, 2, cp, produce7)
        pieces8, size8 = cb.shape[1], cb.shape[2]
        w8, count8 = tiles(cols_b, 256)
        kt8, _ = tiles(cols_a, 512)

        def produce8(n):
            j, i = n // count8, n % count8
            if i == 0:
                keep_transposed(
                    h, cols_a, kt8,
                    lambda k: fc[h, j, k * kt8:(k + 1) * kt8] - cp[h, j, k * kt8:(k + 1) * kt8],
                )
            value = transposed_tile(
                lambda k: ci[j, k * kt8:(k + 1) * kt8, i * w8:(i + 1) * w8], cols_a, kt8, w8, h
            )
            for m in range(w8 // size8):
                cb[h, n * (w8 // size8) + m] = value[m * size8:(m + 1) * size8]

        yield from chain(h, 3, cb, cbx, produce8, w8 // size8)
        for i in range(pieces8):
            j, k = i // (pieces8 // 2), i % (pieces8 // 2)
            child_out[j, k * size8:(k + 1) * size8, lanes] = cbx[h, 0, i] + cb[h, i] + cbx[h, 1, i]

    running = [program(h) for h in range(CHUNKS)]
    turn = 0

    def advance(thread):
        try:
            next(thread)
            return True
        except StopIteration:
            return False

    while any(p is not None for p in running) or side:
        for h in range(CHUNKS):
            if running[h] is not None and turn >= h * OFFSET:
                if not advance(running[h]):
                    running[h] = None
                if turn == 0:
                    route()
            for item in list(side):
                if item[0] == h and turn % GAP == h % GAP and not advance(item[1]):
                    side.remove(item)
        turn += 1
    for h in range(CHUNKS):
        flush(h)


def hand_over(root_in, child_in, root_out, child_out, root_held, child_held, sems):
    loads, stores = [], []
    for k, (src, held, dst) in enumerate(((root_in, root_held, root_out), (child_in, child_held, child_out))):
        axis = len(src.shape) - 2
        size = src.shape[axis] // COPIES
        for i in range(COPIES):
            at = (slice(None),) * axis + (pl.ds(i * size, size),)
            loads.append(pltpu.make_async_copy(src.at[at], held.at[at], sems.at[0, k, i]))
            stores.append(pltpu.make_async_copy(held.at[at], dst.at[at], sems.at[1, k, i]))
    for load in loads:
        load.start()
    for load, store in zip(loads, stores):
        load.wait()
        store.start()
    for store in stores:
        store.wait()


def per_device(nb, nr, child_inverse, child_rhs, child_update, targets, root_inverse, root_rhs):
    bits = nb.bit_length() - 1
    _, cols_a, cols_b = child_inverse.shape
    nl = child_update.shape[1]
    rows_a, own = root_inverse.shape
    R = root_rhs.shape[1]
    H, C = CHUNKS, R // CHUNKS
    cap = 2 * nl // nb
    assert rows_a == 2 * cols_a and nl == LANES
    slots = 2 * nb * cap
    root_pieces = min(PIECES, own // 32)
    child_pieces = 2 * min(PIECES // 2, cols_b // 32)
    most = max(root_pieces, child_pieces, 2)
    any_, vmem = pl.BlockSpec(memory_space=pl.ANY), pl.BlockSpec(memory_space=pltpu.VMEM)

    def sums(*dims):
        return pltpu.VMEM((H, 2, *dims, C), f32)

    def chains(pieces, rows):
        return [pltpu.VMEM((H, pieces, rows, C), f32), pltpu.VMEM((H, 4, pieces, rows, C), f32)]

    results = pl.pallas_call(
        functools.partial(kernel, nb, nr, (cols_a, cols_b, own, rows_a, nl, cap)),
        out_shape=(
            jax.ShapeDtypeStruct(root_rhs.shape, f32),
            jax.ShapeDtypeStruct(child_rhs.shape, f32),
        ),
        in_specs=[any_, any_, any_, vmem, any_, any_],
        out_specs=(vmem, vmem),
        scratch_shapes=[
            pltpu.VMEM(child_inverse.shape, f32),
            pltpu.VMEM(child_update.shape, f32),
            pltpu.VMEM(root_inverse.shape, f32),
            pltpu.VMEM(child_rhs.shape, f32),
            pltpu.VMEM(root_rhs.shape, f32),
            sums(cols_a),
            sums(cols_a // 2),
            sums(cols_a // 2),
            sums(cols_a),
            sums(rows_a // 2),
            sums(cols_a),
            *chains(SMALL, 2 * nl // SMALL),
            *chains(SMALL, 2 * nl // SMALL),
            *chains(root_pieces, own // root_pieces),
            *chains(child_pieces, 2 * cols_b // child_pieces),
            *[pltpu.VMEM((H, slots, C), f32)] * 4,
            pltpu.VMEM((LANES, LANES), f32),
            pltpu.VMEM((slots, 2 * nl), bf16),
            pltpu.VMEM((2 * nl, slots), bf16),
            pltpu.VMEM((own, slots), bf16),
            pltpu.VMEM((slots, own), bf16),
            pltpu.VMEM((H, max(own, cols_a, cols_b, slots), 2 * C), bf16),
            pltpu.VMEM((H, own, 2 * C), bf16),
            pltpu.VMEM((H, 2 * C, max(rows_a, cols_a, nl)), bf16),
            pltpu.SemaphoreType.DMA((5,)),
            pltpu.SemaphoreType.DMA((H, 3, 2, 2 * bits)),
            pltpu.SemaphoreType.DMA((H, 3, 2, 2 * bits)),
            pltpu.SemaphoreType.DMA((H, 2, nb)),
            pltpu.SemaphoreType.DMA((H, 2, nb)),
            pltpu.SemaphoreType.DMA((H, 4, 2, most)),
            pltpu.SemaphoreType.DMA((H, 4, 2, most)),
        ],
        compiler_params=pltpu.CompilerParams(
            collective_id=0, has_side_effects=True, vmem_limit_bytes=62 * 1024 * 1024
        ),
    )(child_inverse, child_rhs, child_update, targets, root_inverse, root_rhs)
    if COPIES == 0:
        return results
    return pl.pallas_call(
        hand_over,
        out_shape=tuple(jax.ShapeDtypeStruct(r.shape, f32) for r in results),
        in_specs=[any_, any_],
        out_specs=(any_, any_),
        scratch_shapes=[
            *[pltpu.VMEM(r.shape, f32) for r in results],
            pltpu.SemaphoreType.DMA((2, 2, COPIES)),
        ],
    )(*results)


def solution(mesh):
    return jax.shard_map(
        functools.partial(per_device, mesh.shape["bulk"], mesh.shape["row"]),
        mesh=mesh,
        in_specs=(
            P(None, "row", "bulk"),
            P(None, "bulk", None),
            P(None, "bulk", "row"),
            P(),
            P("row", "bulk"),
            P("bulk", None),
        ),
        out_specs=(P("bulk", None), P(None, "bulk", None)),
        check_vma=False,
    )
```

```python
import functools

import jax
import jax.numpy as jnp
from jax import lax
from jax.experimental import pallas as pl
from jax.experimental.pallas import tpu as pltpu
from jax.sharding import PartitionSpec as P

MESH = pl.DeviceIdType.MESH
CHUNKS = 2
OFFSET = 0
LATE = (1, 1)
GAP = 1
COPIES = 4
PASSES = 3
SMALL = 1
TM = 512
PIECES = 4
LANES = 128
f32, bf16, i32 = jnp.float32, jnp.bfloat16, jnp.int32


def split(x):
    high = x.astype(bf16)
    return high, (x - high.astype(f32)).astype(bf16)


def dot(a, b):
    return jnp.dot(a, b, preferred_element_type=f32)


def iota(shape, axis):
    return lax.broadcasted_iota(i32, shape, axis)


def one_hot(hit):
    return jnp.where(hit, 1.0, 0.0).astype(bf16)


def log2(n):
    assert n & (n - 1) == 0
    return n.bit_length() - 1


def kernel(
    nb, nr, dims,
    ci_hbm, crhs_hbm, cu_hbm, targets_ref, ri_hbm, rrhs_hbm,
    root_out, child_out,
    ci, cu, ri, crhs_ref, rrhs_ref,
    part, pair, add_r, fc, fr, cp,
    up, upx, fe, fex, bk, bkx, cb, cbx,
    pk1, rv1, pk2, rv2,
    ids, pack, place, spread, pick,
    rhs_w, rhs_x, tmp_t,
    load_sem, ar_s, ar_r, a2a_s, a2a_r, ch_s, ch_r,
):
    bits = log2(nb)
    me = lax.axis_index("bulk")
    row = lax.axis_index("row")
    C = fc.shape[-1]
    cols_a, cols_b, own, rows_a, nl, cap = dims
    orders = (list(range(1, bits)), list(range(1, bits))[::-1])

    loads = [
        pltpu.make_async_copy(ci_hbm, ci, load_sem.at[0]),
        pltpu.make_async_copy(cu_hbm, cu, load_sem.at[1]),
        pltpu.make_async_copy(ri_hbm, ri, load_sem.at[2]),
        pltpu.make_async_copy(crhs_hbm, crhs_ref, load_sem.at[3]),
        pltpu.make_async_copy(rrhs_hbm, rrhs_ref, load_sem.at[4]),
    ]
    loads[3].start()
    loads[0].start()

    def bit_of(bit):
        return (me // (1 << bit)) % 2

    def across(bit):
        return me + (1 << bit) * (1 - 2 * bit_of(bit))

    right = lax.rem(row + 1, nr)
    left = lax.rem(row + nr - 1, nr)
    barrier = pltpu.get_barrier_semaphore()
    for d in range(1, nb):
        pl.semaphore_signal(barrier, inc=1, device_id={"bulk": lax.rem(me + d, nb)}, device_id_type=MESH)
    for side in (left, right):
        pl.semaphore_signal(barrier, inc=1, device_id={"row": side}, device_id_type=MESH)

    def remote(src, dst, send, recv, **where):
        return pltpu.make_async_remote_copy(
            src_ref=src, dst_ref=dst, send_sem=send, recv_sem=recv, device_id=where, device_id_type=MESH
        )

    for x in (upx, fex, bkx, cbx):
        for end, where in enumerate((0, nr - 1)):
            @pl.when(row == where)
            def _():
                for h in range(CHUNKS):
                    x[h, end] = jnp.zeros(x.shape[2:], f32)

    pending = [[] for _ in range(CHUNKS)]

    def flush(h):
        for finish in pending[h]:
            finish()
        pending[h] = []

    def all_reduce(h, which, out, produce):
        half = part.shape[2] // 2
        mine = pl.multiple_of((me % 2) * half, half)
        theirs = pl.multiple_of((1 - me % 2) * half, half)
        sends = []

        def send(f, step, src, dst, bit):
            copy = remote(src, dst, ar_s.at[h, which, f, step], ar_r.at[h, which, f, step], bulk=across(bit))
            copy.start()
            sends.append(copy.wait_send)
            return copy

        def rows(start, length):
            return pl.ds(pl.multiple_of(start, length), length)

        flush(h)
        pairs = []
        for f in range(2):
            produce(f, theirs, half)
            pairs.append(send(f, 0, part.at[h, f, pl.ds(theirs, half)], pair.at[h, f], 0))
        starts, flights, length, off = [mine, mine], [None, None], half, 0

        def halve(f, step):
            n, bit = length // 2, bit_of(orders[f][step])
            flights[f] = send(
                f, 1 + step, part.at[h, f, rows(starts[f] + (1 - bit) * n, n)], add_r.at[h, f, pl.ds(off, n)],
                orders[f][step],
            )
            starts[f] = starts[f] + bit * n

        for f in range(2):
            produce(f, mine, half)
            pairs[f].wait_recv()
            part[h, f, pl.ds(mine, half)] += pair[h, f]
            halve(f, 0)
        yield
        for step in range(bits - 1):
            length //= 2
            for f in range(2):
                flights[f].wait_recv()
                at = rows(starts[f], length)
                total = part[h, f, at] + add_r[h, f, pl.ds(off, length)]
                if step < bits - 2:
                    part[h, f, at] = total
                    off += length
                    halve(f, step + 1)
                    off -= length
                else:
                    out[h, f, at] = total
                    at = out.at[h, f, at]
                    flights[f] = send(f, bits, at, at, orders[f][step])
            off += length
            yield
        for step in reversed(range(bits - 1)):
            for f in range(2):
                flights[f].wait_recv()
                starts[f] = starts[f] - bit_of(orders[f][step]) * length
                at = out.at[h, f, rows(starts[f], 2 * length)]
                to = orders[f][step - 1] if step > 0 else 0
                flights[f] = send(f, 2 * bits - 1 - step, at, at, to)
            length *= 2
            yield
        for f in range(2):
            flights[f].wait_recv()
        pending[h] += sends

    def exchange(h, which, packed, arrived):
        n = 2 * cap
        here = pl.ds(pl.multiple_of(me * n, n), n)
        copies = []
        for d in range(1, nb):
            peer = lax.rem(me + d, nb)
            copy = remote(
                packed.at[h, pl.ds(pl.multiple_of(peer * n, n), n)], arrived.at[h, here],
                a2a_s.at[h, which, d], a2a_r.at[h, which, d], bulk=peer,
            )
            copy.start()
            copies.append(copy)
        arrived[h, here] = packed[h, here]
        yield
        for copy in copies:
            copy.wait_recv()
        pending[h] += [copy.wait_send for copy in copies]

    def chain(h, which, p, x, produce=None, stride=1):
        pieces = p.shape[1]

        def flow(side, i, has_source, has_target, target):
            copy = remote(
                x.at[h, 2 + side, i], x.at[h, side, i],
                ch_s.at[h, which, side, i], ch_r.at[h, which, side, i], row=target,
            )

            @pl.when(has_source)
            def _():
                copy.wait_recv()

            @pl.when(has_target)
            def _():
                x[h, 2 + side, i] = x[h, side, i] + p[h, i]
                copy.start()

        for t in range(pieces + nr - 1):
            if t > 0:
                yield
            if produce is not None and t < pieces and t % stride == 0:
                produce(t // stride)
            i = t - row

            @pl.when((i >= 0) & (i < pieces))
            def _():
                flow(0, i, row > 0, row < nr - 1, right)

            k = t - (nr - 1 - row)

            @pl.when((k >= 0) & (k < pieces))
            def _():
                flow(1, k, row < nr - 1, row > 0, left)

        def finish():
            for i in range(pieces):
                for side, has_target, target in ((0, row < nr - 1, right), (1, row > 0, left)):
                    @pl.when(has_target)
                    def _():
                        remote(
                            x.at[h, 2 + side, i], x.at[h, side, i],
                            ch_s.at[h, which, side, i], ch_r.at[h, which, side, i], row=target,
                        ).wait_send()

        pending[h].append(finish)

    def times(a_tile, count, store, h, width, w=rhs_w):
        def body(i, carry):
            high, low = split(a_tile(i))
            both = dot(high, w[h, :width])
            if PASSES == 3:
                store(i, both[:, :C] + (both[:, C:] + dot(low, w[h, :width, :C])))
            else:
                both += dot(low, w[h, :width])
                store(i, both[:, :C] + both[:, C:])
            return carry

        lax.fori_loop(0, count, body, 0)

    def moved(rows, store, h, width, tile=256):
        tile = min(tile, rows.shape[0])

        def body(i, carry):
            at = pl.ds(pl.multiple_of(i * tile, tile), tile)
            both = dot(rows[at], rhs_w[h, :width])
            store(at, both[:, :C] + both[:, C:])
            return carry

        lax.fori_loop(0, rows.shape[0] // tile, body, 0)

    def keep_right(h, at, value, w=rhs_w):
        high, low = split(value)
        w[h, at, :C] = high
        w[h, at, C:] = low

    def keep_transposed(h, depth, k_tile, y_tile):
        for k in range(depth // k_tile):
            high, low = split(y_tile(k).T)
            tmp_t[h, :C, k * k_tile:(k + 1) * k_tile] = high
            tmp_t[h, C:, k * k_tile:(k + 1) * k_tile] = low

    def transposed_tile(a_tile, depth, k_tile, width, h):
        total = jnp.zeros((2 * C, width), f32)
        extra = jnp.zeros((C, width), f32)
        for k in range(depth // k_tile):
            high, low = split(a_tile(k))
            y = tmp_t[h, :, k * k_tile:(k + 1) * k_tile]
            total += dot(y, high)
            if PASSES == 3:
                extra += dot(y[:C], low)
            else:
                total += dot(y, low)
        return (total[:C] + (total[C:] + extra)).T

    def tiles(n, most):
        size = min(n, most)
        return size, n // size

    slots = nb * 2 * cap

    def turned(line):
        return jnp.broadcast_to(line, (LANES, LANES)).T

    def route():
        square = (LANES, LANES)
        before = iota(square, 0) < iota(square, 1)
        ids[...] = jnp.full(ids.shape, -1.0, f32)
        for j in range(2):
            for b in range(nb):
                ids[j * nb + b:j * nb + b + 1, :] = targets_ref[j:j + 1, b * nl:(b + 1) * nl].astype(f32)
        for j in range(2):
            line = ids[pl.ds(j * nb + me, 1), :]
            owner = lax.shift_right_logical(line.astype(i32), log2(own)).astype(f32)
            same = (turned(owner) == owner) & before
            rank = jnp.sum(jnp.where(same, 1.0, 0.0), axis=0, keepdims=True)
            position = owner * (2.0 * cap) + (rank + j * cap)
            column = turned(position).astype(i32)
            at = slice(j * nl, (j + 1) * nl)
            pack[:, at] = one_hot(iota((slots, nl), 0) == position.astype(i32))
            for g in range(slots // LANES):
                place[at, g * LANES:(g + 1) * LANES] = one_hot(iota(square, 1) + g * LANES == column)
        first = (me * own).astype(f32)
        local = ids[...] - first
        inside = (local >= 0.0) & (local < float(own))
        ones = jnp.where(inside, 1.0, 0.0).astype(bf16)
        rank = dot(ones, one_hot(before))
        index = iota(ids.shape, 0)
        child = jnp.where(index >= nb, 1, 0)
        base = (index - nb * child) * (2 * cap) + child * cap
        position = jnp.where(inside, rank + base.astype(f32), -1.0)
        position, local = position.T, local.T
        fill = iota(square, 1).astype(f32)
        lines = []
        for g in range(slots // LANES):
            total = jnp.zeros(square, f32)
            for j in range(2):
                for b in range(nb):
                    if (b * 2 * cap + j * cap) // LANES == g:
                        r = j * nb + b
                        hit = position[:, r:r + 1] == fill + float(g * LANES)
                        total = total + jnp.where(hit, local[:, r:r + 1] + 1.0, 0.0)
            lines.append(jnp.sum(total, axis=0, keepdims=True) - 1.0)
        for g, line in enumerate(lines):
            at = slice(g * LANES, (g + 1) * LANES)
            spread[:, at] = one_hot(iota((own, LANES), 0) == line.astype(i32))
            column = turned(line).astype(i32)
            for k in range(own // LANES):
                pick[at, k * LANES:(k + 1) * LANES] = one_hot(iota(square, 1) + k * LANES == column)

    def seat(j):
        if SMALL == 1:
            return 0, slice(j * nl, (j + 1) * nl)
        return j, slice(0, nl)

    side = []

    def deliver(h):
        yield from chain(h, 2, bk, bkx)
        size = bk.shape[2]
        for i in range(bk.shape[1]):
            root_out[i * size:(i + 1) * size, h * C:(h + 1) * C] = bkx[h, 0, i] + bk[h, i] + bkx[h, 1, i]

    def program(h):
        lanes = slice(h * C, (h + 1) * C)
        if h == 0:
            pl.semaphore_wait(barrier, nb + 1)
            loads[3].wait()
            loads[0].wait()
            loads[1].start()
            loads[4].start()
            loads[2].start()

        def produce1(j, start, length):
            tm, count = tiles(length, TM)
            keep_right(h, slice(0, cols_b), crhs_ref[j, :, lanes])

            def store(i, value):
                part[h, j, pl.ds(pl.multiple_of(start + i * tm, tm), tm)] = value

            times(lambda i: ci[j, pl.ds(pl.multiple_of(start + i * tm, tm), tm), :], count, store, h, cols_b)

        yield from all_reduce(h, 0, fc, produce1)
        if h == 0:
            loads[1].wait()
            loads[4].wait()
        for j in range(2):
            keep_right(h, slice(0, cols_a), fc[h, j])

            def store(i, value, j=j):
                up[(h, *seat(j))] = value

            times(lambda i, j=j: cu[j], 1, store, h, cols_a)
        flush(h)
        yield from chain(h, 0, up, upx)
        for j in range(2):
            keep_right(h, slice(j * nl, (j + 1) * nl), upx[(h, 0, *seat(j))] + up[(h, *seat(j))] + upx[(h, 1, *seat(j))])

        def store_packed(at, value):
            pk1[h, at] = value

        moved(pack, store_packed, h, 2 * nl)
        yield from exchange(h, 0, pk1, rv1)
        keep_right(h, slice(0, slots), rv1[h])

        def store_rest(at, value):
            keep_right(h, at, rrhs_ref[at, lanes] - value, rhs_x)

        moved(spread, store_rest, h, slots)
        if h == 0:
            loads[2].wait()
        per = rows_a // 2

        def produce4(f, start, length):
            tm, count = tiles(length, TM)

            def store(i, value):
                part[h, f, pl.ds(pl.multiple_of(start + i * tm, tm), tm)] = value

            times(lambda i: ri[pl.ds(pl.multiple_of(f * per + start + i * tm, tm), tm), :], count, store, h, own, rhs_x)

        yield from all_reduce(h, 1, fr, produce4)
        pieces, size = bk.shape[1], bk.shape[2]
        width = min(256, own)
        kt5, _ = tiles(per, 512)
        halves = per // kt5

        keep_transposed(h, rows_a, kt5, lambda k: fr[h, k // halves, (k % halves) * kt5:(k % halves + 1) * kt5])

        for i in range(own // width):
            value = transposed_tile(
                lambda k: ri[k * kt5:(k + 1) * kt5, i * width:(i + 1) * width], rows_a, kt5, width, h
            )
            for n in range(width // size):
                bk[h, i * (width // size) + n] = value[n * size:(n + 1) * size]
            keep_right(h, slice(i * width, (i + 1) * width), value)
        flush(h)

        def store_picked(at, value):
            pk2[h, at] = value

        moved(pick, store_picked, h, own)
        if LATE[h] == 0:
            side.append((h, deliver(h)))
        yield from exchange(h, 1, pk2, rv2)
        keep_right(h, slice(0, slots), rv2[h])

        for j in range(2):
            both = dot(place[j * nl:(j + 1) * nl], rhs_w[h, :slots])
            fe[(h, *seat(j))] = both[:, :C] + both[:, C:]
        yield from chain(h, 1, fe, fex)
        if LATE[h] == 1:
            side.append((h, deliver(h)))

        def produce7(j, start, length):
            w7, count7 = tiles(length, 256)
            keep_transposed(h, nl, nl, lambda k: fex[(h, 0, *seat(j))] + fe[(h, *seat(j))] + fex[(h, 1, *seat(j))])

            def body(i, carry):
                at = pl.ds(pl.multiple_of(start + i * w7, w7), w7)
                part[h, j, at] = transposed_tile(lambda k: cu[j, :, at], nl, nl, w7, h)
                return carry

            lax.fori_loop(0, count7, body, 0)

        yield from all_reduce(h, 2, cp, produce7)
        pieces8, size8 = cb.shape[1], cb.shape[2]
        w8, count8 = tiles(cols_b, 256)
        kt8, _ = tiles(cols_a, 512)

        def produce8(n):
            j, i = n // count8, n % count8
            if i == 0:
                keep_transposed(
                    h, cols_a, kt8,
                    lambda k: fc[h, j, k * kt8:(k + 1) * kt8] - cp[h, j, k * kt8:(k + 1) * kt8],
                )
            value = transposed_tile(
                lambda k: ci[j, k * kt8:(k + 1) * kt8, i * w8:(i + 1) * w8], cols_a, kt8, w8, h
            )
            for m in range(w8 // size8):
                cb[h, n * (w8 // size8) + m] = value[m * size8:(m + 1) * size8]

        yield from chain(h, 3, cb, cbx, produce8, w8 // size8)
        for i in range(pieces8):
            j, k = i // (pieces8 // 2), i % (pieces8 // 2)
            child_out[j, k * size8:(k + 1) * size8, lanes] = cbx[h, 0, i] + cb[h, i] + cbx[h, 1, i]

    running = [program(h) for h in range(CHUNKS)]
    turn = 0

    def advance(thread):
        try:
            next(thread)
            return True
        except StopIteration:
            return False

    while any(p is not None for p in running) or side:
        for h in range(CHUNKS):
            if running[h] is not None and turn >= h * OFFSET:
                if not advance(running[h]):
                    running[h] = None
                if turn == 0 and h == CHUNKS - 1:
                    route()
            for item in list(side):
                if item[0] == h and turn % GAP == h % GAP and not advance(item[1]):
                    side.remove(item)
        turn += 1
    for h in range(CHUNKS):
        flush(h)


def hand_over(root_in, child_in, root_out, child_out, root_held, child_held, sems):
    loads, stores = [], []
    for k, (src, held, dst) in enumerate(((root_in, root_held, root_out), (child_in, child_held, child_out))):
        axis = len(src.shape) - 2
        size = src.shape[axis] // COPIES
        for i in range(COPIES):
            at = (slice(None),) * axis + (pl.ds(i * size, size),)
            loads.append(pltpu.make_async_copy(src.at[at], held.at[at], sems.at[0, k, i]))
            stores.append(pltpu.make_async_copy(held.at[at], dst.at[at], sems.at[1, k, i]))
    for load in loads:
        load.start()
    for load, store in zip(loads, stores):
        load.wait()
        store.start()
    for store in stores:
        store.wait()


def per_device(nb, nr, child_inverse, child_rhs, child_update, targets, root_inverse, root_rhs):
    bits = nb.bit_length() - 1
    _, cols_a, cols_b = child_inverse.shape
    nl = child_update.shape[1]
    rows_a, own = root_inverse.shape
    R = root_rhs.shape[1]
    H, C = CHUNKS, R // CHUNKS
    cap = 2 * nl // nb
    assert rows_a == 2 * cols_a and nl == LANES
    slots = 2 * nb * cap
    root_pieces = min(PIECES, own // 32)
    child_pieces = 2 * min(PIECES // 2, cols_b // 32)
    most = max(root_pieces, child_pieces, 2)
    any_, vmem = pl.BlockSpec(memory_space=pl.ANY), pl.BlockSpec(memory_space=pltpu.VMEM)

    def sums(*dims):
        return pltpu.VMEM((H, 2, *dims, C), f32)

    def chains(pieces, rows):
        return [pltpu.VMEM((H, pieces, rows, C), f32), pltpu.VMEM((H, 4, pieces, rows, C), f32)]

    results = pl.pallas_call(
        functools.partial(kernel, nb, nr, (cols_a, cols_b, own, rows_a, nl, cap)),
        out_shape=(
            jax.ShapeDtypeStruct(root_rhs.shape, f32),
            jax.ShapeDtypeStruct(child_rhs.shape, f32),
        ),
        in_specs=[any_, any_, any_, vmem, any_, any_],
        out_specs=(vmem, vmem),
        scratch_shapes=[
            pltpu.VMEM(child_inverse.shape, f32),
            pltpu.VMEM(child_update.shape, f32),
            pltpu.VMEM(root_inverse.shape, f32),
            pltpu.VMEM(child_rhs.shape, f32),
            pltpu.VMEM(root_rhs.shape, f32),
            sums(cols_a),
            sums(cols_a // 2),
            sums(cols_a // 2),
            sums(cols_a),
            sums(rows_a // 2),
            sums(cols_a),
            *chains(SMALL, 2 * nl // SMALL),
            *chains(SMALL, 2 * nl // SMALL),
            *chains(root_pieces, own // root_pieces),
            *chains(child_pieces, 2 * cols_b // child_pieces),
            *[pltpu.VMEM((H, slots, C), f32)] * 4,
            pltpu.VMEM((LANES, LANES), f32),
            pltpu.VMEM((slots, 2 * nl), bf16),
            pltpu.VMEM((2 * nl, slots), bf16),
            pltpu.VMEM((own, slots), bf16),
            pltpu.VMEM((slots, own), bf16),
            pltpu.VMEM((H, max(own, cols_a, cols_b, slots), 2 * C), bf16),
            pltpu.VMEM((H, own, 2 * C), bf16),
            pltpu.VMEM((H, 2 * C, max(rows_a, cols_a, nl)), bf16),
            pltpu.SemaphoreType.DMA((5,)),
            pltpu.SemaphoreType.DMA((H, 3, 2, 2 * bits)),
            pltpu.SemaphoreType.DMA((H, 3, 2, 2 * bits)),
            pltpu.SemaphoreType.DMA((H, 2, nb)),
            pltpu.SemaphoreType.DMA((H, 2, nb)),
            pltpu.SemaphoreType.DMA((H, 4, 2, most)),
            pltpu.SemaphoreType.DMA((H, 4, 2, most)),
        ],
        compiler_params=pltpu.CompilerParams(
            collective_id=0, has_side_effects=True, vmem_limit_bytes=62 * 1024 * 1024
        ),
    )(child_inverse, child_rhs, child_update, targets, root_inverse, root_rhs)
    if COPIES == 0:
        return results
    return pl.pallas_call(
        hand_over,
        out_shape=tuple(jax.ShapeDtypeStruct(r.shape, f32) for r in results),
        in_specs=[any_, any_],
        out_specs=(any_, any_),
        scratch_shapes=[
            *[pltpu.VMEM(r.shape, f32) for r in results],
            pltpu.SemaphoreType.DMA((2, 2, COPIES)),
        ],
    )(*results)


def solution(mesh):
    return jax.shard_map(
        functools.partial(per_device, mesh.shape["bulk"], mesh.shape["row"]),
        mesh=mesh,
        in_specs=(
            P(None, "row", "bulk"),
            P(None, "bulk", None),
            P(None, "bulk", "row"),
            P(),
            P("row", "bulk"),
            P("bulk", None),
        ),
        out_specs=(P("bulk", None), P(None, "bulk", None)),
        check_vma=False,
    )
```
